32 devices in a mesh: fsdp: 4 (over x, core), ctx: 2 (over y), tensor: 4 (over z).
Axes of the slice: x: 2, y: 2, z: 4, core: 2. Of those that a mesh axis runs over, the one named last changes fastest.
Arguments:
- frames_in: bfloat16 [16, 1024, 768], P('fsdp', ('ctx', 'tensor')), may hold values from -6 to 6
- out_cotangent: bfloat16 [16, 1024, 768], P('fsdp', ('ctx', 'tensor')), may hold values from -6 to 6
- attend_weight: float32 [3, 768, 768], P(None, ('fsdp', 'ctx'), 'tensor'), as said below
- output_weight: float32 [768, 768], P('tensor', ('fsdp', 'ctx')), may hold values from -0.875 to 0.875
- up_weight: float32 [768, 3072], P(('fsdp', 'ctx'), 'tensor'), may hold values from -0.21875 to 0.21875
- down_weight: float32 [3072, 768], P('tensor', ('fsdp', 'ctx')), may hold values from -0.109375 to 0.109375
- vectors: float32 [12, 768], replicated, as said below
- attend_mean: float32 [3, 768, 768], P(None, ('fsdp', 'ctx'), 'tensor'), may hold values from -24 to 24
- attend_square: float32 [3, 768, 768], P(None, ('fsdp', 'ctx'), 'tensor'), may hold values from 0.32768 to 1.6384
- output_mean: float32 [768, 768], P('tensor', ('fsdp', 'ctx')), may hold values from -24 to 24
- output_square: float32 [768, 768], P('tensor', ('fsdp', 'ctx')), may hold values from 0.32768 to 1.6384
- up_mean: float32 [768, 3072], P(('fsdp', 'ctx'), 'tensor'), may hold values from -24 to 24
- up_square: float32 [768, 3072], P(('fsdp', 'ctx'), 'tensor'), may hold values from 0.32768 to 1.6384
- down_mean: float32 [3072, 768], P('tensor', ('fsdp', 'ctx')), may hold values from -24 to 24
- down_square: float32 [3072, 768], P('tensor', ('fsdp', 'ctx')), may hold values from 0.32768 to 1.6384
- vector_mean: float32 [12, 768], replicated, may hold values from -80 to 80
- vector_square: float32 [12, 768], replicated, may hold values from 3.2768 to 32.768
Outputs:
- frames_out: bfloat16 [16, 1024, 768], P('fsdp', ('ctx', 'tensor'))
- frames_grad: float32 [16, 1024, 768], P('fsdp', ('ctx', 'tensor'))
- attend_grad: float32 [3, 768, 768], P(None, ('fsdp', 'ctx'), 'tensor')
- output_grad: float32 [768, 768], P('tensor', ('fsdp', 'ctx'))
- up_grad: float32 [768, 3072], P(('fsdp', 'ctx'), 'tensor')
- down_grad: float32 [3072, 768], P('tensor', ('fsdp', 'ctx'))
- vector_grad: float32 [12, 768], replicated
- attend_new: float32 [3, 768, 768], P(None, ('fsdp', 'ctx'), 'tensor')
- output_new: float32 [768, 768], P('tensor', ('fsdp', 'ctx'))
- up_new: float32 [768, 3072], P(('fsdp', 'ctx'), 'tensor')
- down_new: float32 [3072, 768], P('tensor', ('fsdp', 'ctx'))
- vector_new: float32 [12, 768], replicated
- attend_mean_new: float32 [3, 768, 768], P(None, ('fsdp', 'ctx'), 'tensor')
- attend_square_new: float32 [3, 768, 768], P(None, ('fsdp', 'ctx'), 'tensor')
- output_mean_new: float32 [768, 768], P('tensor', ('fsdp', 'ctx'))
- output_square_new: float32 [768, 768], P('tensor', ('fsdp', 'ctx'))
- up_mean_new: float32 [768, 3072], P(('fsdp', 'ctx'), 'tensor')
- up_square_new: float32 [768, 3072], P(('fsdp', 'ctx'), 'tensor')
- down_mean_new: float32 [3072, 768], P('tensor', ('fsdp', 'ctx'))
- down_square_new: float32 [3072, 768], P('tensor', ('fsdp', 'ctx'))
- vector_mean_new: float32 [12, 768], replicated
- vector_square_new: float32 [12, 768], replicated
The draws below stay inside these ranges and needn't reach their ends.
Inputs may be any that keep to these rules, and one draw needn't show every extreme that they name: `attend_weight`: the three stacked projections of query, key and value; entries are of order 768 ** -0.5. `vectors`: rows 0 and 5 are the two norms' gains, between 0.4 and 1.6; the other rows are biases of order one.
All inputs are finite; a program needn't handle non-finite values.
Results may differ from the reference program's by a relative error of at most 0.007.
The reference program's roundings to bfloat16 on the way count: a program that leaves them out, or rounds other values in their place, can miss the bound.
Values may be sent and summed in bfloat16 or wider, within the bound.
No kernel may reach another device: no remote copies, remote signals or barrier semaphores. Data moves between devices by JAX's collectives and lax.ppermute only.
A program may use at most 128 MiB of HBM per device.

```python
import math
import jax
import jax.numpy as jnp
from jax import lax

D = 768
H = 12
FF = 3072
HD = 64
FRAMES = 1024
STEP = 3
CLIPS = 16
TOKENS = 16384


def draw_attend_weight(key, part):
    baseline = jax.random.normal(jax.random.fold_in(key, 1), (3, D, D), jnp.float32)
    return baseline * D ** (-0.5)


def draw_vectors(key, part):
    row_index = jnp.arange(12)[:, None]
    is_gain = (row_index == 0) | (row_index == 5)
    spread = jnp.clip(jax.random.normal(key, (12, D), jnp.float32) * 0.5, -1.5, 1.5)
    return jnp.where(is_gain, 1.0 + 0.4 * spread, spread)


def steps_of(rng, dims, pieces, smallest, high):
    def one(dim, blocks):
        heights = jax.random.uniform(jax.random.fold_in(jax.random.fold_in(rng, 6), dim), (blocks,), jnp.float32, smallest / len(pieces), high / len(pieces))
        return jnp.repeat(jnp.exp(heights), dims[dim] // blocks).reshape((-1,) + (1,) * (len(dims) - dim - 1))

    factor_of = one(*pieces[0])
    for cut in pieces[1:]:
        factor_of = factor_of * one(*cut)
    return factor_of


def noise(key, dims, scale, bound, pieces=(), kind=jnp.bfloat16):
    entries = jax.random.normal(key, dims, jnp.float32) * scale
    if len(pieces) > 0:
        entries = steps_of(key, dims, pieces, -0.22, 0.18) * entries
    return jnp.clip(entries, min=-bound, max=bound).astype(kind)


def setup_inputs(seed: int = 0) -> dict:
    keys = jax.random.split(jax.random.key(seed), 18)
    return {
        "frames_in": noise(keys[0], (CLIPS, FRAMES, D), 1.0, 6.0, ((0, 4), (1, 8))),
        "out_cotangent": noise(keys[1], (CLIPS, FRAMES, D), 1.0, 6.0, ((0, 4), (1, 8))),
        "attend_weight": draw_attend_weight(jax.random.fold_in(keys[17], 71), 0),
        "output_weight": noise(keys[3], (D, D), (max(D // 16, 1)) ** -0.5, 0.875, ((0, 4), (1, 8)), jnp.float32),
        "up_weight": noise(keys[4], (D, FF), D ** -0.5, 0.21875, ((0, 8), (1, 4)), jnp.float32),
        "down_weight": noise(keys[5], (FF, D), FF ** -0.5, 0.109375, ((0, 4), (1, 8)), jnp.float32),
        "vectors": draw_vectors(jax.random.fold_in(keys[17], 71), 0),
        "attend_mean": noise(keys[7], (3, D, D), (0.03 * TOKENS ** 0.5), 24.0, ((1, 8), (2, 4)), jnp.float32),
        "attend_square": jnp.clip(jnp.exp(math.log(1.6384) - 1.609438 * jax.random.uniform(keys[8], (3, D, D), jnp.float32) ** steps_of(keys[8], (3, D, D), ((1, 8), (2, 4)), -0.2, 0.2)), 0.32768, 1.6384),
        "output_mean": noise(keys[9], (D, D), (0.03 * TOKENS ** 0.5), 24.0, ((0, 4), (1, 8)), jnp.float32),
        "output_square": jnp.clip(jnp.exp(math.log(1.6384) - 1.609438 * jax.random.uniform(keys[10], (D, D), jnp.float32) ** steps_of(keys[10], (D, D), ((0, 4), (1, 8)), -0.2, 0.2)), 0.32768, 1.6384),
        "up_mean": noise(keys[11], (D, FF), (0.03 * TOKENS ** 0.5), 24.0, ((0, 8), (1, 4)), jnp.float32),
        "up_square": jnp.clip(jnp.exp(math.log(1.6384) - 1.609438 * jax.random.uniform(keys[12], (D, FF), jnp.float32) ** steps_of(keys[12], (D, FF), ((0, 8), (1, 4)), -0.2, 0.2)), 0.32768, 1.6384),
        "down_mean": noise(keys[13], (FF, D), (0.03 * TOKENS ** 0.5), 24.0, ((0, 4), (1, 8)), jnp.float32),
        "down_square": jnp.clip(jnp.exp(math.log(1.6384) - 1.609438 * jax.random.uniform(keys[14], (FF, D), jnp.float32) ** steps_of(keys[14], (FF, D), ((0, 4), (1, 8)), -0.2, 0.2)), 0.32768, 1.6384),
        "vector_mean": noise(keys[15], (12, D), (0.1 * TOKENS ** 0.5), 80.0, (), jnp.float32),
        "vector_square": jnp.clip(jnp.exp(jax.random.uniform(keys[16], (12, D), jnp.float32, math.log(3.2768), math.log(32.768))), 3.2768, 32.768),
    }


norm_eps = 1e-05
learn_rate = 0.04
beta_one = 0.9
beta_two = 0.999
adam_eps = 1e-08
decay_rate = 0.01
root_half = 0.7071067811865476
inv_root_tau = 0.3989422804014327

def layer_norm(inputs, gain_row, shift_row):
    row_mean = lax.optimization_barrier(jnp.mean(inputs, -1, keepdims=True))
    centred = inputs - row_mean
    variance = lax.optimization_barrier(jnp.mean(centred * centred, -1, keepdims=True))
    inv_scale = lax.rsqrt(variance + norm_eps)
    normed = centred * inv_scale
    return (normed * gain_row + shift_row, normed, inv_scale)

def norm_back(upstream, normed, inv_scale, gain_row):
    dnormed = upstream * gain_row
    mean_one = lax.optimization_barrier(jnp.mean(dnormed, -1, keepdims=True))
    mean_two = lax.optimization_barrier(jnp.mean(dnormed * normed, -1, keepdims=True))
    return inv_scale * (dnormed - mean_one - normed * mean_two)

def gelu_value(pre_act):
    return 0.5 * pre_act * (1.0 + jax.scipy.special.erf(pre_act * root_half))

def gelu_slope(pre_act):
    return 0.5 * (1.0 + jax.scipy.special.erf(pre_act * root_half)) + pre_act * jnp.exp(-0.5 * pre_act * pre_act) * inv_root_tau

def adamw(weight_now, gradient, mean_old, square_old, decay):
    mean_new = beta_one * mean_old + (1.0 - beta_one) * gradient
    square_new = beta_two * square_old + (1.0 - beta_two) * gradient * gradient
    mean_hat = mean_new / (1.0 - beta_one ** STEP)
    square_hat = square_new / (1.0 - beta_two ** STEP)
    weight_new = weight_now - learn_rate * (mean_hat / (jnp.sqrt(square_hat) + adam_eps) + decay * weight_now)
    return (weight_new, mean_new, square_new)

def reference(frames_in, out_cotangent, attend_weight, output_weight, up_weight, down_weight, vectors, attend_mean, attend_square, output_mean, output_square, up_mean, up_square, down_mean, down_square, vector_mean, vector_square):
    attend_low = attend_weight.astype(jnp.bfloat16)
    output_low = output_weight.astype(jnp.bfloat16)
    up_low = up_weight.astype(jnp.bfloat16)
    down_low = down_weight.astype(jnp.bfloat16)
    score_scale = HD ** (-0.5)
    hidden_bias = vectors[8:12].reshape(FF)

    def clip_step(carry, blocks):
        frames_clip, cot_clip = blocks
        inputs = frames_clip.astype(jnp.float32)
        norm_out1, normed1, inv_one = layer_norm(inputs, vectors[0], vectors[1])
        in_norm1 = norm_out1.astype(jnp.bfloat16)
        projected = jnp.einsum('fd,tde->tfe', in_norm1.astype(jnp.float32), attend_low.astype(jnp.float32))
        queries = (projected[0] + vectors[2]).astype(jnp.bfloat16)
        key_rows = projected[1].astype(jnp.bfloat16)
        val_rows = (projected[2] + vectors[3]).astype(jnp.bfloat16)
        query_heads = queries.reshape(FRAMES, H, HD).astype(jnp.float32)
        key_heads = key_rows.reshape(FRAMES, H, HD).astype(jnp.float32)
        value_heads = val_rows.reshape(FRAMES, H, HD).astype(jnp.float32)
        scores = jnp.einsum('qhe,khe->hqk', query_heads, key_heads) * score_scale
        row_max = lax.optimization_barrier(jnp.max(scores, -1, keepdims=True))
        log_total = row_max + jnp.log(lax.optimization_barrier(jnp.sum(jnp.exp(scores - row_max), -1, keepdims=True)))
        probs_full = jnp.exp(scores - log_total)
        attn_probs = probs_full.astype(jnp.bfloat16)
        context = jnp.einsum('hqk,khe->qhe', attn_probs.astype(jnp.float32), value_heads).astype(jnp.bfloat16)
        context_flat = context.reshape(FRAMES, D)
        residual = inputs + jnp.dot(context_flat, output_low, preferred_element_type=jnp.float32) + vectors[4]
        norm_out2, normed2, inv_two = layer_norm(residual, vectors[5], vectors[6])
        in_norm2 = norm_out2.astype(jnp.bfloat16)
        pre_act = jnp.dot(in_norm2, up_low, preferred_element_type=jnp.float32) + hidden_bias
        hidden = gelu_value(pre_act).astype(jnp.bfloat16)
        result = residual + jnp.dot(hidden, down_low, preferred_element_type=jnp.float32) + vectors[7]
        cotangent = cot_clip.astype(jnp.float32)
        grad_c2 = lax.optimization_barrier(jnp.sum(cotangent, 0))
        grad_down = jnp.dot(hidden.T, cot_clip, preferred_element_type=jnp.float32)
        dhidden = jnp.dot(cot_clip, down_low.T, preferred_element_type=jnp.float32)
        dpre = dhidden * gelu_slope(pre_act)
        grad_c1 = lax.optimization_barrier(jnp.sum(dpre, 0))
        dpre_low = dpre.astype(jnp.bfloat16)
        grad_up = jnp.dot(in_norm2.T, dpre_low, preferred_element_type=jnp.float32)
        dnorm2 = jnp.dot(dpre_low, up_low.T, preferred_element_type=jnp.float32)
        dresidual = cotangent + norm_back(dnorm2, normed2, inv_two, vectors[5])
        grad_g2 = lax.optimization_barrier(jnp.sum(dnorm2 * normed2, 0))
        grad_b2 = lax.optimization_barrier(jnp.sum(dnorm2, 0))
        grad_bo = lax.optimization_barrier(jnp.sum(dresidual, 0))
        dres_low = dresidual.astype(jnp.bfloat16)
        grad_output = jnp.dot(context_flat.T, dres_low, preferred_element_type=jnp.float32)
        dcontext = jnp.dot(dres_low, output_low.T, preferred_element_type=jnp.float32).astype(jnp.bfloat16)
        dcontext_heads = dcontext.reshape(FRAMES, H, HD).astype(jnp.float32)
        dvalue = jnp.einsum('hqk,qhe->khe', attn_probs.astype(jnp.float32), dcontext_heads)
        dprobs = jnp.einsum('qhe,khe->hqk', dcontext_heads, value_heads)
        delta = lax.optimization_barrier(jnp.sum(dcontext_heads * context.astype(jnp.float32), -1))
        dscores = (probs_full * (dprobs - delta.T[:, :, None]) * score_scale).astype(jnp.bfloat16).astype(jnp.float32)
        dquery = jnp.einsum('hqk,khe->qhe', dscores, key_heads).reshape(FRAMES, D)
        dkey = jnp.einsum('hqk,qhe->khe', dscores, query_heads).reshape(FRAMES, D)
        dvalue = dvalue.reshape(FRAMES, D)
        grad_bq = lax.optimization_barrier(jnp.sum(dquery, 0))
        grad_bv = lax.optimization_barrier(jnp.sum(dvalue, 0))
        dproj = jnp.stack([dquery, dkey, dvalue]).astype(jnp.bfloat16).astype(jnp.float32)
        grad_attend = jnp.einsum('fd,tfe->tde', in_norm1.astype(jnp.float32), dproj)
        dnorm1 = jnp.einsum('tfe,tde->fd', dproj, attend_low.astype(jnp.float32))
        dinputs = dresidual + norm_back(dnorm1, normed1, inv_one, vectors[0])
        grad_g1 = lax.optimization_barrier(jnp.sum(dnorm1 * normed1, 0))
        grad_b1 = lax.optimization_barrier(jnp.sum(dnorm1, 0))
        grad_vec = jnp.concatenate([jnp.stack([grad_g1, grad_b1, grad_bq, grad_bv, grad_bo, grad_g2, grad_b2, grad_c2]), grad_c1.reshape(4, D)], 0)
        new_carry = (carry[0] + grad_attend, carry[1] + grad_output, carry[2] + grad_up, carry[3] + grad_down, carry[4] + grad_vec)
        return (new_carry, (result.astype(jnp.bfloat16), dinputs))
    start = (jnp.zeros((3, D, D), jnp.float32), jnp.zeros((D, D), jnp.float32), jnp.zeros((D, FF), jnp.float32), jnp.zeros((FF, D), jnp.float32), jnp.zeros((12, D), jnp.float32))
    totals, stacked = lax.scan(clip_step, start, (frames_in, out_cotangent))
    frames_out, frames_grad = stacked
    attend_grad, output_grad, up_grad, down_grad, vector_grad = totals
    attend_new, attend_mean_new, attend_square_new = adamw(attend_weight, attend_grad, attend_mean, attend_square, decay_rate)
    output_new, output_mean_new, output_square_new = adamw(output_weight, output_grad, output_mean, output_square, decay_rate)
    up_new, up_mean_new, up_square_new = adamw(up_weight, up_grad, up_mean, up_square, decay_rate)
    down_new, down_mean_new, down_square_new = adamw(down_weight, down_grad, down_mean, down_square, decay_rate)
    vector_new, vector_mean_new, vector_square_new = adamw(vectors, vector_grad, vector_mean, vector_square, 0.0)
    return (frames_out, frames_grad, attend_grad, output_grad, up_grad, down_grad, vector_grad, attend_new, output_new, up_new, down_new, vector_new, attend_mean_new, attend_square_new, output_mean_new, output_square_new, up_mean_new, up_square_new, down_mean_new, down_square_new, vector_mean_new, vector_square_new)
```

```python
import jax
import jax.numpy as jnp
from jax import lax
from jax.experimental import pallas as pl
from jax.experimental.pallas import tpu as pltpu
from jax.sharding import PartitionSpec as P

HD = 64
STEP = 3
CORES = 2

norm_eps = 1e-05
learn_rate = 0.04
beta_one = 0.9
beta_two = 0.999
adam_eps = 1e-08
decay_rate = 0.01
root_half = 0.7071067811865476
inv_root_tau = 0.3989422804014327

AXES = ("fsdp", "ctx", "tensor")
f32 = jnp.float32
bf16 = jnp.bfloat16


def layer_norm(inputs, gain_row, shift_row):
    row_mean = jnp.mean(inputs, -1, keepdims=True)
    centred = inputs - row_mean
    variance = jnp.mean(centred * centred, -1, keepdims=True)
    inv_scale = lax.rsqrt(variance + norm_eps)
    normed = centred * inv_scale
    return (normed * gain_row + shift_row, normed, inv_scale)


def norm_back(upstream, normed, inv_scale, gain_row):
    dnormed = upstream * gain_row
    mean_one = jnp.mean(dnormed, -1, keepdims=True)
    mean_two = jnp.mean(dnormed * normed, -1, keepdims=True)
    return inv_scale * (dnormed - mean_one - normed * mean_two)


def adamw(weight_now, gradient, mean_old, square_old, decay):
    mean_new = beta_one * mean_old + (1.0 - beta_one) * gradient
    square_new = beta_two * square_old + (1.0 - beta_two) * gradient * gradient
    mean_hat = mean_new / (1.0 - beta_one**STEP)
    square_hat = square_new / (1.0 - beta_two**STEP)
    weight_new = weight_now - learn_rate * (
        mean_hat / (jnp.sqrt(square_hat) + adam_eps) + decay * weight_now
    )
    return (weight_new, mean_new, square_new)


def dot(a, b, ca, cb):
    return lax.dot_general(a, b, (((ca,), (cb,)), ((), ())), preferred_element_type=f32)


def attend_forward_body(q_ref, ka_ref, va_ref, kb_ref, vb_ref, o_ref, lse_ref):
    lane = lax.broadcasted_iota(jnp.int32, (1, 2 * HD), 1)
    queries = q_ref[...]
    val_t = (va_ref[...].T, vb_ref[...].T)
    parts = []
    for head in range(2):
        mask = ((lane // HD) == head).astype(f32) * HD ** (-0.5)
        q_head = queries * mask.astype(bf16)
        s_a = dot(ka_ref[...], q_head, 1, 1)
        s_b = dot(kb_ref[...], q_head, 1, 1)
        top = jnp.maximum(
            jnp.max(s_a, 0, keepdims=True), jnp.max(s_b, 0, keepdims=True)
        )
        e_a = jnp.exp(s_a - top)
        e_b = jnp.exp(s_b - top)
        total = jnp.sum(e_a, 0, keepdims=True) + jnp.sum(e_b, 0, keepdims=True)
        lse_ref[0, head : head + 1, :] = top + jnp.log(total)
        inv = 1.0 / total
        rows = slice(head * HD, (head + 1) * HD)
        parts.append(
            dot(val_t[0][rows], (e_a * inv).astype(bf16), 1, 0)
            + dot(val_t[1][rows], (e_b * inv).astype(bf16), 1, 0)
        )
    o_ref[...] = jnp.concatenate(parts, 0).T.astype(bf16)


def attend_forward(queries, key_a, val_a, key_b, val_b):
    rows, width = queries.shape
    pairs = width // (2 * HD)
    block = pl.BlockSpec((rows, 2 * HD), lambda i: (0, i))
    return pl.pallas_call(
        attend_forward_body,
        grid=(pairs,),
        in_specs=[block] * 5,
        out_specs=[block, pl.BlockSpec((1, 2, rows), lambda i: (i, 0, 0))],
        out_shape=[
            jax.ShapeDtypeStruct((rows, width), bf16),
            jax.ShapeDtypeStruct((pairs, 2, rows), f32),
        ],
        cost_estimate=pl.CostEstimate(
            flops=8 * rows * rows * width,
            transcendentals=2 * rows * rows * width // HD,
            bytes_accessed=12 * rows * width,
        ),
        name="attend_forward",
    )(queries, key_a, val_a, key_b, val_b)


def attend_backward_body(
    q_ref,
    ka_ref,
    va_ref,
    kb_ref,
    vb_ref,
    o_ref,
    do_ref,
    lse_ref,
    dq_ref,
    dka_ref,
    dva_ref,
    dkb_ref,
    dvb_ref,
    sums_ref,
):
    lane = lax.broadcasted_iota(jnp.int32, (1, 2 * HD), 1)
    queries = q_ref[...]
    dcontext = do_ref[...]
    weighed = (dcontext.astype(f32) * o_ref[...].astype(f32)).T
    key_t = (ka_ref[...].T, kb_ref[...].T)
    dkeys = [None, None]
    dvals = [None, None]
    dq_parts = []
    for head in range(2):
        mask = ((lane // HD) == head).astype(f32)
        q_head = queries * (mask * HD ** (-0.5)).astype(bf16)
        do_head = dcontext * mask.astype(bf16)
        rows = slice(head * HD, (head + 1) * HD)
        delta = jnp.sum(weighed[rows], 0, keepdims=True)
        lse = lse_ref[0, head : head + 1, :]
        dq_head = None
        for part, (k_ref, v_ref) in enumerate(((ka_ref, va_ref), (kb_ref, vb_ref))):
            probs = jnp.exp(dot(k_ref[...], q_head, 1, 1) - lse)
            dprobs = dot(v_ref[...], do_head, 1, 1)
            dscores = (probs * (dprobs - delta)).astype(bf16)
            dval = dot(probs.astype(bf16), do_head, 1, 0)
            dkey = dot(dscores, q_head, 1, 0)
            dq_part = dot(key_t[part][rows], dscores, 1, 0)
            dvals[part] = dval if head == 0 else dvals[part] + dval
            dkeys[part] = dkey if head == 0 else dkeys[part] + dkey
            dq_head = dq_part if part == 0 else dq_head + dq_part
        dq_parts.append(dq_head)
    dquery = jnp.concatenate(dq_parts, 0).T * HD ** (-0.5)
    dq_ref[...] = dquery.astype(bf16)
    dka_ref[...] = dkeys[0]
    dkb_ref[...] = dkeys[1]
    dva_ref[...] = dvals[0]
    dvb_ref[...] = dvals[1]
    sums_ref[0:1, :] = jnp.sum(dquery, 0, keepdims=True)
    sums_ref[1:2, :] = jnp.sum(dvals[0], 0, keepdims=True) + jnp.sum(dvals[1], 0, keepdims=True)


def attend_backward(queries, key_a, val_a, key_b, val_b, context, dcontext, lse):
    rows, width = queries.shape
    pairs = width // (2 * HD)
    block = pl.BlockSpec((rows, 2 * HD), lambda i: (0, i))
    return pl.pallas_call(
        attend_backward_body,
        grid=(pairs,),
        in_specs=[block] * 7 + [pl.BlockSpec((1, 2, rows), lambda i: (i, 0, 0))],
        out_specs=[block] * 5 + [pl.BlockSpec((2, 2 * HD), lambda i: (0, i))],
        out_shape=[jax.ShapeDtypeStruct((rows, width), bf16)]
        + [jax.ShapeDtypeStruct((rows, width), f32)] * 4
        + [jax.ShapeDtypeStruct((2, width), f32)],
        cost_estimate=pl.CostEstimate(
            flops=20 * rows * rows * width,
            transcendentals=2 * rows * rows * width // HD,
            bytes_accessed=32 * rows * width,
        ),
        name="attend_backward",
    )(queries, key_a, val_a, key_b, val_b, context, dcontext, lse)


def hidden_body(
    h_ref,
    e_ref,
    x_ref,
    up_ref,
    down_ref,
    c1_ref,
    c2_ref,
    out_ref,
    dh_ref,
    dup_ref,
    ddown_ref,
    dc1_ref,
    h_t,
    e_t,
    total,
):
    step = pl.program_id(0)

    @pl.when(step == 0)
    def _():
        h_t[...] = h_ref[...].T
        e_t[...] = e_ref[...].T
        total[...] = x_ref[...] + c2_ref[...]
        dh_ref[...] = jnp.zeros_like(dh_ref)

    pre_act = dot(h_ref[...], up_ref[0], 1, 0) + c1_ref[0]
    half = 0.5 * (1.0 + lax.erf(pre_act * root_half))
    hidden = (pre_act * half).astype(bf16)
    slope = half + pre_act * jnp.exp(-0.5 * pre_act * pre_act) * inv_root_tau
    total[...] += dot(hidden, down_ref[0], 1, 1)
    dpre = dot(e_ref[...], down_ref[0], 1, 0) * slope
    dc1_ref[0] = jnp.sum(dpre, 0, keepdims=True)
    dpre_low = dpre.astype(bf16)
    ddown_ref[0] = dot(e_t[...], hidden, 1, 0).astype(bf16)
    dup_ref[0] = dot(h_t[...], dpre_low, 1, 0).astype(bf16)
    dh_ref[...] += dot(dpre_low, up_ref[0], 1, 1)

    @pl.when(step == pl.num_programs(0) - 1)
    def _():
        out_ref[...] = total[...].astype(bf16)


def hidden_both(h_low, cot, residual, up, down, c1_rows, c2_row):
    rows, width = h_low.shape
    blocks, _, units = up.shape
    whole = pl.BlockSpec((rows, width), lambda i: (0, 0))
    weight = pl.BlockSpec((1, width, units), lambda i: (i, 0, 0))
    bias = pl.BlockSpec((1, 1, units), lambda i: (i, 0, 0))
    return pl.pallas_call(
        hidden_body,
        grid=(blocks,),
        in_specs=[whole, whole, whole, weight, weight, bias, pl.BlockSpec((1, width), lambda i: (0, 0))],
        out_specs=[whole, whole, weight, weight, bias],
        out_shape=[
            jax.ShapeDtypeStruct((rows, width), bf16),
            jax.ShapeDtypeStruct((rows, width), f32),
            jax.ShapeDtypeStruct(up.shape, bf16),
            jax.ShapeDtypeStruct(up.shape, bf16),
            jax.ShapeDtypeStruct((blocks, 1, units), f32),
        ],
        scratch_shapes=[
            pltpu.VMEM((width, rows), bf16),
            pltpu.VMEM((width, rows), bf16),
            pltpu.VMEM((rows, width), f32),
        ],
        cost_estimate=pl.CostEstimate(
            flops=12 * rows * width * units * blocks,
            transcendentals=2 * rows * units * blocks,
            bytes_accessed=8 * width * units * blocks + 14 * rows * width,
        ),
        name="hidden_both",
    )(h_low, cot, residual, up, down, c1_rows[:, None, :], c2_row[None])


class Grid:
    def __init__(self):
        self.fsdp = lax.axis_size("fsdp")
        self.outer = self.fsdp // CORES
        self.ctx = lax.axis_size("ctx")
        self.tensor = lax.axis_size("tensor")
        here = lax.axis_index("fsdp")
        self.fo = here // CORES
        self.core = lax.rem(here, CORES)
        self.y = lax.axis_index("ctx")
        self.z = lax.axis_index("tensor")

    def index(self, fo, core, y, z):
        return ((fo * CORES + core) * self.ctx + y) * self.tensor + z

    def move(self, data, target):
        pairs = []
        for fo in range(self.outer):
            for core in range(CORES):
                for y in range(self.ctx):
                    for z in range(self.tensor):
                        pairs.append((self.index(fo, core, y, z), self.index(*target(fo, core, y, z))))
        return jax.tree.map(lambda leaf: lax.ppermute(leaf, AXES, pairs), data)

    def from_outer(self, data, j):
        return self.move(data, lambda f, c, y, z: ((f - j) % self.outer, c, y, z))

    def to_outer(self, data, j):
        return self.move(data, lambda f, c, y, z: ((f + j) % self.outer, c, y, z))

    def from_ctx(self, data, j):
        return self.move(data, lambda f, c, y, z: (f, c, (y - j) % self.ctx, z))

    def to_ctx(self, data, j):
        return self.move(data, lambda f, c, y, z: (f, c, (y + j) % self.ctx, z))

    def from_tensor(self, data, j):
        return self.move(data, lambda f, c, y, z: (f, c, y, (z - j) % self.tensor))

    def to_tensor(self, data, j):
        return self.move(data, lambda f, c, y, z: (f, c, y, (z + j) % self.tensor))

    def other_core(self, data):
        return self.move(data, lambda f, c, y, z: (f, 1 - c, y, z))


def place(pieces, start, axis):
    count = len(pieces)
    if count == 1:
        return jnp.expand_dims(pieces[0], axis)
    row = jnp.stack(list(pieces) + list(pieces[:-1]), axis)
    return lax.dynamic_slice_in_dim(row, lax.rem(count - start, count), count, axis)


def pick(data, index, axis):
    return lax.dynamic_index_in_dim(data, index, axis, False)


def spread(grid, planes, order):
    for axis in order:
        if axis == "y":
            pieces = [planes] + [grid.from_ctx(planes, j) for j in range(1, grid.ctx)]
            planes = place(pieces, grid.y, planes.ndim - 2)
        else:
            pieces = [planes] + [grid.from_outer(planes, j) for j in range(1, grid.outer)]
            planes = place(pieces, grid.fo, 1)
    planes = place([planes, grid.other_core(planes)], grid.core, 2)
    return planes.reshape(planes.shape[0], -1, planes.shape[-1])


def collect(grid, grads, order):
    count, rows, width = grads.shape
    grads = grads.reshape(
        count, grid.outer, CORES, grid.ctx, rows // (grid.fsdp * grid.ctx), width
    )
    arrived = grid.other_core(pick(grads, 1 - grid.core, 2))
    total = pick(grads, grid.core, 2).astype(f32) + arrived.astype(f32)
    for axis in order:
        if axis == "x":
            sums = pick(total, grid.fo, 1)
            for j in range(1, grid.outer):
                out = pick(total, lax.rem(grid.fo + j, grid.outer), 1).astype(bf16)
                sums = sums + grid.to_outer(out, j).astype(f32)
        else:
            dim = total.ndim - 3
            sums = pick(total, grid.y, dim)
            for j in range(1, grid.ctx):
                out = pick(total, lax.rem(grid.y + j, grid.ctx), dim).astype(bf16)
                sums = sums + grid.to_ctx(out, j).astype(f32)
        total = sums
    return total


def to_owner(grid, blocks):
    total = blocks[0]
    for j in range(1, grid.tensor):
        total = total + grid.to_tensor(blocks[j].astype(bf16), j).astype(f32)
    return total


def sum_everywhere(grid, rows):
    rows = rows + grid.other_core(rows)
    step = 1
    while step < grid.outer:
        rows = rows + grid.move(rows, lambda f, c, y, z: (f ^ step, c, y, z))
        step *= 2
    step = 1
    while step < grid.ctx:
        rows = rows + grid.move(rows, lambda f, c, y, z: (f, c, y ^ step, z))
        step *= 2
    step = 1
    while step < grid.tensor:
        rows = rows + grid.move(rows, lambda f, c, y, z: (f, c, y, z ^ step))
        step *= 2
    return rows


def clips_in(grid, frames):
    pieces = []
    for j in range(grid.tensor):
        out = pick(frames, lax.rem(grid.z + j, grid.tensor), 0)
        pieces.append(
            grid.move(out, lambda f, c, y, z: (f, y, c, (z + j) % grid.tensor))
        )
    return jnp.concatenate(pieces, 0)


def clips_out(grid, rows):
    step = rows.shape[0] // grid.tensor
    pieces = []
    for j in range(grid.tensor):
        out = rows[j * step : (j + 1) * step]
        pieces.append(
            grid.move(out, lambda f, c, y, z: (f, y, c, (z - j) % grid.tensor))
        )
    return place(pieces, grid.z, 0)


def per_device(
    frames_in,
    out_cotangent,
    attend_weight,
    output_weight,
    up_weight,
    down_weight,
    vectors,
    attend_mean,
    attend_square,
    output_mean,
    output_square,
    up_mean,
    up_square,
    down_mean,
    down_square,
    vector_mean,
    vector_square,
):
    grid = Grid()
    width = frames_in.shape[2]
    part = attend_weight.shape[2]

    def turn(rows, back=False):
        count = rows.shape[0]
        start = lax.rem(count - grid.z, count) if back else grid.z
        return lax.dynamic_slice_in_dim(jnp.concatenate([rows, rows], 0), start, count, 0)

    x_low = clips_in(grid, frames_in)

    def columns(shard):
        return [shard] + [grid.from_tensor(shard, j) for j in range(1, grid.tensor)]

    proj = jnp.concatenate(columns(attend_weight.astype(bf16)), 2)
    output_t = jnp.concatenate(columns(output_weight.astype(bf16).T[None]), 2)
    up = jnp.stack(columns(up_weight.astype(bf16)))
    down_t = jnp.stack(columns(down_weight.astype(bf16).T))

    proj_full = jnp.concatenate(
        [spread(grid, proj[:2], "yx"), spread(grid, proj[2:], "xy")], 0
    )
    output_full = spread(grid, output_t, "xy")[0]
    up_full = spread(grid, up, "yx")
    down_full = spread(grid, down_t, "xy")
    cot_low = clips_in(grid, out_cotangent)

    bias_query = turn(vectors[2].reshape(grid.tensor, part)).reshape(width)
    bias_value = turn(vectors[3].reshape(grid.tensor, part)).reshape(width)
    hidden_bias = turn(vectors[8:12].reshape(grid.tensor, -1))

    inputs = x_low.astype(f32)
    norm_out1, normed1, inv_one = layer_norm(inputs, vectors[0], vectors[1])
    in_norm1 = norm_out1.astype(bf16)
    queries = (dot(in_norm1, proj_full[0], 1, 0) + bias_query).astype(bf16)
    key_a = dot(in_norm1, proj_full[1], 1, 0).astype(bf16)
    val_a = (dot(in_norm1, proj_full[2], 1, 0) + bias_value).astype(bf16)
    key_b, val_b = grid.other_core((key_a, val_a))
    context, log_total = attend_forward(queries, key_a, val_a, key_b, val_b)
    residual = inputs + dot(context, output_full, 1, 1) + vectors[4]
    norm_out2, normed2, inv_two = layer_norm(residual, vectors[5], vectors[6])
    in_norm2 = norm_out2.astype(bf16)

    result, dnorm2, grad_up, grad_down, grad_c1 = hidden_both(
        in_norm2, cot_low, residual, up_full, down_full, hidden_bias, vectors[7]
    )
    frames_out = clips_out(grid, result)

    cotangent = cot_low.astype(f32)
    dresidual = cotangent + norm_back(dnorm2, normed2, inv_two, vectors[5])
    dres_low = dresidual.astype(bf16)
    dcontext = dot(dres_low, output_full, 1, 0).astype(bf16)
    grad_output = dot(dres_low, context, 0, 0).astype(bf16)
    early = jnp.concatenate(
        [
            jnp.stack(
                [
                    jnp.sum(dresidual, 0),
                    jnp.sum(dnorm2 * normed2, 0),
                    jnp.sum(dnorm2, 0),
                    jnp.sum(cotangent, 0),
                ]
            ),
            turn(grad_c1[:, 0, :], True).reshape(-1, width),
        ],
        0,
    )
    early = sum_everywhere(grid, early)

    dquery, dkey_a, dval_a, dkey_b, dval_b, sums = attend_backward(
        queries, key_a, val_a, key_b, val_b, context, dcontext, log_total
    )
    dkey_in, dval_in = grid.other_core((dkey_b, dval_b))
    dproj = (
        dquery,
        (dkey_a + dkey_in).astype(bf16),
        (dval_a + dval_in).astype(bf16),
    )
    grad_attend = [dot(in_norm1, each, 0, 0).astype(bf16)[None] for each in dproj]
    dnorm1 = sum(dot(dproj[i], proj_full[i], 1, 1) for i in range(3))
    dinputs = dresidual + norm_back(dnorm1, normed1, inv_one, vectors[0])
    frames_grad = clips_out(grid, dinputs.astype(bf16)).astype(f32)
    sums = turn(sums.reshape(2, grid.tensor, part).transpose(1, 0, 2), True)
    late = jnp.concatenate(
        [
            jnp.stack([jnp.sum(dnorm1 * normed1, 0), jnp.sum(dnorm1, 0)]),
            sums.transpose(1, 0, 2).reshape(2, width),
        ],
        0,
    )
    late = sum_everywhere(grid, late)

    def blocks_of(total):
        return [total[..., j * part : (j + 1) * part] for j in range(grid.tensor)]

    up_grad = to_owner(grid, list(collect(grid, grad_up, "xy")))
    down_grad = to_owner(grid, list(collect(grid, grad_down, "yx"))).T
    output_grad = to_owner(grid, blocks_of(collect(grid, grad_output[None], "yx")[0])).T
    attend_grad = to_owner(
        grid,
        blocks_of(
            jnp.concatenate(
                [
                    collect(grid, jnp.concatenate(grad_attend[:2], 0), "xy"),
                    collect(grid, grad_attend[2], "yx"),
                ],
                0,
            )
        ),
    )
    vector_grad = jnp.concatenate([late, early], 0)

    attend_new, attend_mean_new, attend_square_new = adamw(
        attend_weight, attend_grad, attend_mean, attend_square, decay_rate
    )
    output_new, output_mean_new, output_square_new = adamw(
        output_weight, output_grad, output_mean, output_square, decay_rate
    )
    up_new, up_mean_new, up_square_new = adamw(up_weight, up_grad, up_mean, up_square, decay_rate)
    down_new, down_mean_new, down_square_new = adamw(
        down_weight, down_grad, down_mean, down_square, decay_rate
    )
    vector_new, vector_mean_new, vector_square_new = adamw(
        vectors, vector_grad, vector_mean, vector_square, 0.0
    )
    return (
        frames_out,
        frames_grad,
        attend_grad,
        output_grad,
        up_grad,
        down_grad,
        vector_grad,
        attend_new,
        output_new,
        up_new,
        down_new,
        vector_new,
        attend_mean_new,
        attend_square_new,
        output_mean_new,
        output_square_new,
        up_mean_new,
        up_square_new,
        down_mean_new,
        down_square_new,
        vector_mean_new,
        vector_square_new,
    )


def solution(mesh):
    frames = P("fsdp", ("ctx", "tensor"), None)
    attend = P(None, ("fsdp", "ctx"), "tensor")
    tall = P("tensor", ("fsdp", "ctx"))
    flat = P(("fsdp", "ctx"), "tensor")
    weights = (attend, tall, flat, tall)
    return jax.shard_map(
        per_device,
        mesh=mesh,
        in_specs=(frames, frames)
        + weights
        + (P(), attend, attend, tall, tall, flat, flat, tall, tall, P(), P()),
        out_specs=(frames, frames)
        + weights
        + (P(),)
        + weights
        + (P(), attend, attend, tall, tall, flat, flat, tall, tall, P(), P()),
        check_vma=False,
    )
```

```python
import jax
import jax.numpy as jnp
from jax import lax
from jax.experimental import pallas as pl
from jax.experimental.pallas import tpu as pltpu
from jax.sharding import PartitionSpec as P


HD = 64
STEP = 3
CORES = 2

norm_eps = 1e-05
learn_rate = 0.04
beta_one = 0.9
beta_two = 0.999
adam_eps = 1e-08
decay_rate = 0.01
root_half = 0.7071067811865476
inv_root_tau = 0.3989422804014327

AXES = ("fsdp", "ctx", "tensor")
f32 = jnp.float32
bf16 = jnp.bfloat16


def layer_norm(inputs, gain_row, shift_row):
    row_mean = jnp.mean(inputs, -1, keepdims=True)
    centred = inputs - row_mean
    variance = jnp.mean(centred * centred, -1, keepdims=True)
    inv_scale = lax.rsqrt(variance + norm_eps)
    normed = centred * inv_scale
    return (normed * gain_row + shift_row, normed, inv_scale)


def norm_back(upstream, normed, inv_scale, gain_row):
    dnormed = upstream * gain_row
    mean_one = jnp.mean(dnormed, -1, keepdims=True)
    mean_two = jnp.mean(dnormed * normed, -1, keepdims=True)
    return inv_scale * (dnormed - mean_one - normed * mean_two)


def adamw(weight_now, gradient, mean_old, square_old, decay):
    mean_new = beta_one * mean_old + (1.0 - beta_one) * gradient
    square_new = beta_two * square_old + (1.0 - beta_two) * gradient * gradient
    mean_hat = mean_new / (1.0 - beta_one**STEP)
    square_hat = square_new / (1.0 - beta_two**STEP)
    weight_new = weight_now - learn_rate * (
        mean_hat / (jnp.sqrt(square_hat) + adam_eps) + decay * weight_now
    )
    return (weight_new, mean_new, square_new)


def dot(a, b, ca, cb):
    return lax.dot_general(a, b, (((ca,), (cb,)), ((), ())), preferred_element_type=f32)


def add_dot(total, a, b, ca, cb):
    part = dot(a, b, ca, cb)
    return part if total is None else total + part


class Layout:
    def __init__(self, outer, ctx, rows):
        self.outer, self.ctx, self.rows = outer, ctx, rows
        self.count = outer * ctx
        self.total = self.count * CORES * rows

    def offset(self, place, ctx_first, other, j):
        if ctx_first:
            jy, jf = j % self.ctx, j // self.ctx
        else:
            jf, jy = j % self.outer, j // self.outer
        block = ((place[0] ^ jf) * CORES + (place[1] ^ other)) * self.ctx + (place[2] ^ jy)
        return pl.multiple_of(block * self.rows, self.rows)

    def scratch(self, width):
        kind = bf16 if self.rows % 16 == 0 else f32
        return pltpu.VMEM((self.total, width), kind)

    def join(self, place, ctx_first, mine, theirs, plane, target):
        for other, ref in enumerate((mine, theirs)):
            for j in range(self.count):
                rows = pl.ds(self.offset(place, ctx_first, other, j), self.rows)
                target[rows, :] = ref[j, plane].astype(target.dtype)

    def cut(self, place, ctx_first, source, mine, theirs, plane):
        for other, ref in enumerate((mine, theirs)):
            for j in range(self.count):
                rows = pl.ds(self.offset(place, ctx_first, other, j), self.rows)
                ref[j, plane] = source[rows, :].astype(bf16)


def whole(*shape):
    return pl.BlockSpec(shape, lambda i, s: (0,) * len(shape))


def call(body, grid, in_specs, out_specs, out_shape, scratch, flops, trans, moved, mib):
    return pl.pallas_call(
        body,
        grid_spec=pltpu.PrefetchScalarGridSpec(
            num_scalar_prefetch=1,
            grid=grid,
            in_specs=in_specs,
            out_specs=out_specs,
            scratch_shapes=scratch,
        ),
        out_shape=out_shape,
        compiler_params=pltpu.CompilerParams(vmem_limit_bytes=mib * 1024 * 1024),
        cost_estimate=pl.CostEstimate(flops=flops, transcendentals=trans, bytes_accessed=moved),
    )


def project_body(
    layout, place, x0, x1, x2, x3, ma, ta, mb, tb, vec_ref, bias_ref, x_ref, h_ref, q_ref, kv_ref, w_ref, joined
):
    count = x0.shape[0]
    for j, ref in enumerate((x0, x1, x2, x3)):
        rows = slice(j * count, (j + 1) * count)
        x_ref[rows, :] = ref[...]
        norm_out, _, _ = layer_norm(ref[...].astype(f32), vec_ref[0:1, :], vec_ref[1:2, :])
        h_ref[rows, :] = norm_out.astype(bf16)
    for plane in range(4):
        first = plane < 2
        layout.join(place, first, ma if first else mb, ta if first else tb, plane % 2, joined)
        weight = joined[...].astype(bf16)
        w_ref[plane] = weight
        if plane == 3:
            break
        out = dot(h_ref[...], weight, 1, 0)
        if plane == 0:
            q_ref[...] = (out + bias_ref[0:1, :]).astype(bf16)
        elif plane == 1:
            kv_ref[0] = out.astype(bf16)
        else:
            kv_ref[1] = (out + bias_ref[1:2, :]).astype(bf16)


def project(layout, place, x_pieces, pieces, vectors, biases):
    step, width = x_pieces[0].shape
    rows = step * len(x_pieces)
    frames = whole(rows, width)
    return call(
        lambda *refs: project_body(layout, *refs),
        (1,),
        [whole(step, width)] * len(x_pieces)
        + [whole(*pieces[0].shape)] * 4
        + [whole(*vectors.shape), whole(*biases.shape)],
        [frames, frames, frames, whole(2, rows, width), whole(4, width, width)],
        [jax.ShapeDtypeStruct((rows, width), bf16)] * 3
        + [
            jax.ShapeDtypeStruct((2, rows, width), bf16),
            jax.ShapeDtypeStruct((4, width, width), bf16),
        ],
        [layout.scratch(width)],
        6 * rows * width * width,
        0,
        16 * width * width + 10 * rows * width,
        32,
    )(place, *x_pieces, *pieces, vectors, biases)


def attend_forward_body(place, q_ref, own_ref, far_ref, o_ref, lse_ref):
    lane = lax.broadcasted_iota(jnp.int32, (1, 2 * HD), 1)
    queries = q_ref[...]
    val_t = (own_ref[1].T, far_ref[1].T)
    parts = []
    for head in range(2):
        mask = ((lane // HD) == head).astype(f32) * HD ** (-0.5)
        q_head = queries * mask.astype(bf16)
        s_a = dot(own_ref[0], q_head, 1, 1)
        s_b = dot(far_ref[0], q_head, 1, 1)
        top = jnp.maximum(
            jnp.max(s_a, 0, keepdims=True), jnp.max(s_b, 0, keepdims=True)
        )
        e_a = jnp.exp(s_a - top)
        e_b = jnp.exp(s_b - top)
        total = jnp.sum(e_a, 0, keepdims=True) + jnp.sum(e_b, 0, keepdims=True)
        lse_ref[0, head : head + 1, :] = top + jnp.log(total)
        inv = 1.0 / total
        rows = slice(head * HD, (head + 1) * HD)
        parts.append(
            dot(val_t[0][rows], (e_a * inv).astype(bf16), 1, 0)
            + dot(val_t[1][rows], (e_b * inv).astype(bf16), 1, 0)
        )
    o_ref[...] = jnp.concatenate(parts, 0).T.astype(bf16)


def attend_forward(place, queries, own, far):
    rows, width = queries.shape
    pairs = width // (2 * HD)
    block = pl.BlockSpec((rows, 2 * HD), lambda i, s: (0, i))
    both = pl.BlockSpec((2, rows, 2 * HD), lambda i, s: (0, 0, i))
    return call(
        attend_forward_body,
        (pairs,),
        [block, both, both],
        [block, pl.BlockSpec((1, 2, rows), lambda i, s: (i, 0, 0))],
        [
            jax.ShapeDtypeStruct((rows, width), bf16),
            jax.ShapeDtypeStruct((pairs, 2, rows), f32),
        ],
        [],
        8 * rows * rows * width,
        2 * rows * rows * width // HD,
        12 * rows * width,
        24,
    )(place, queries, own, far)


def attend_backward_body(
    place,
    q_ref,
    own_ref,
    far_ref,
    o_ref,
    do_ref,
    lse_ref,
    dq_ref,
    dkeep_ref,
    dgive_ref,
    sums_ref,
):
    lane = lax.broadcasted_iota(jnp.int32, (1, 2 * HD), 1)
    queries = q_ref[...]
    dcontext = do_ref[...]
    weighed = (dcontext.astype(f32) * o_ref[...].astype(f32)).T
    key_t = (own_ref[0].T, far_ref[0].T)
    dkeys = [None, None]
    dvals = [None, None]
    dq_parts = []
    for head in range(2):
        mask = ((lane // HD) == head).astype(f32)
        q_head = queries * (mask * HD ** (-0.5)).astype(bf16)
        do_head = dcontext * mask.astype(bf16)
        rows = slice(head * HD, (head + 1) * HD)
        delta = jnp.sum(weighed[rows], 0, keepdims=True)
        lse = lse_ref[0, head : head + 1, :]
        dq_head = None
        for part, ref in enumerate((own_ref, far_ref)):
            probs = jnp.exp(dot(ref[0], q_head, 1, 1) - lse)
            dprobs = dot(ref[1], do_head, 1, 1)
            dscores = (probs * (dprobs - delta)).astype(bf16)
            dvals[part] = add_dot(dvals[part], probs.astype(bf16), do_head, 1, 0)
            dkeys[part] = add_dot(dkeys[part], dscores, q_head, 1, 0)
            dq_head = add_dot(dq_head, key_t[part][rows], dscores, 1, 0)
        dq_parts.append(dq_head)
    dquery = jnp.concatenate(dq_parts, 0).T * HD ** (-0.5)
    dq_ref[...] = dquery.astype(bf16)
    dkeep_ref[0] = dkeys[0]
    dkeep_ref[1] = dvals[0]
    dgive_ref[0] = dkeys[1].astype(bf16)
    dgive_ref[1] = dvals[1].astype(bf16)
    sums_ref[0:1, :] = jnp.sum(dquery, 0, keepdims=True)
    sums_ref[1:2, :] = jnp.sum(dvals[0], 0, keepdims=True) + jnp.sum(dvals[1], 0, keepdims=True)


def attend_backward(place, queries, own, far, context, dcontext, lse):
    rows, width = queries.shape
    pairs = width // (2 * HD)
    block = pl.BlockSpec((rows, 2 * HD), lambda i, s: (0, i))
    both = pl.BlockSpec((2, rows, 2 * HD), lambda i, s: (0, 0, i))
    return call(
        attend_backward_body,
        (pairs,),
        [block, both, both, block, block, pl.BlockSpec((1, 2, rows), lambda i, s: (i, 0, 0))],
        [block, both, both, pl.BlockSpec((2, 2 * HD), lambda i, s: (0, i))],
        [
            jax.ShapeDtypeStruct((rows, width), bf16),
            jax.ShapeDtypeStruct((2, rows, width), f32),
            jax.ShapeDtypeStruct((2, rows, width), bf16),
            jax.ShapeDtypeStruct((2, width), f32),
        ],
        [],
        20 * rows * rows * width,
        2 * rows * rows * width // HD,
        32 * rows * width,
        32,
    )(place, queries, own, far, context, dcontext, lse)


TILE = 512


def tiles(width, *lead):
    return pl.BlockSpec(lead + (TILE, width), lambda i, s: (0,) * len(lead) + (i, 0))


def gather_sums(sums_ref, *rows):
    @pl.when(pl.program_id(0) == 0)
    def _():
        sums_ref[...] = jnp.zeros_like(sums_ref)

    for j, values in enumerate(rows):
        sums_ref[j : j + 1, :] += jnp.sum(values, 0, keepdims=True)


def mix_body(place, x_ref, o_ref, w_ref, vec_ref, x1_ref, h_ref):
    residual = x_ref[...].astype(f32) + dot(o_ref[...], w_ref[0], 1, 1) + vec_ref[4:5, :]
    x1_ref[...] = residual
    norm_out, _, _ = layer_norm(residual, vec_ref[5:6, :], vec_ref[6:7, :])
    h_ref[...] = norm_out.astype(bf16)


def mix(place, x_low, context, weights, vectors):
    rows, width = x_low.shape
    return call(
        mix_body,
        (rows // TILE,),
        [
            tiles(width),
            tiles(width),
            pl.BlockSpec((1, width, width), lambda i, s: (3, 0, 0)),
            whole(*vectors.shape),
        ],
        [tiles(width), tiles(width)],
        [jax.ShapeDtypeStruct((rows, width), f32), jax.ShapeDtypeStruct((rows, width), bf16)],
        [],
        2 * rows * width * width,
        0,
        2 * width * width + 10 * rows * width,
        20,
    )(place, x_low, context, weights, vectors)


def unmix_body(place, dh_ref, x1_ref, e_ref, w_ref, vec_ref, dx_ref, low_ref, do_ref, sums_ref):
    cot = e_ref[...].astype(f32)
    dnorm = dh_ref[...]
    _, normed, inv_scale = layer_norm(x1_ref[...], vec_ref[5:6, :], vec_ref[6:7, :])
    dresidual = cot + norm_back(dnorm, normed, inv_scale, vec_ref[5:6, :])
    dx_ref[...] = dresidual
    low = dresidual.astype(bf16)
    low_ref[...] = low
    do_ref[...] = dot(low, w_ref[0], 1, 0).astype(bf16)
    gather_sums(sums_ref, dresidual, dnorm * normed, dnorm, cot)


def unmix(place, dnorm, residual, cot, weights, vectors):
    rows, width = residual.shape
    return call(
        unmix_body,
        (rows // TILE,),
        [
            tiles(width),
            tiles(width),
            tiles(width),
            pl.BlockSpec((1, width, width), lambda i, s: (3, 0, 0)),
            whole(*vectors.shape),
        ],
        [tiles(width), tiles(width), tiles(width), whole(4, width)],
        [
            jax.ShapeDtypeStruct((rows, width), f32),
            jax.ShapeDtypeStruct((rows, width), bf16),
            jax.ShapeDtypeStruct((rows, width), bf16),
            jax.ShapeDtypeStruct((4, width), f32),
        ],
        [],
        2 * rows * width * width,
        0,
        2 * width * width + 18 * rows * width,
        24,
    )(place, dnorm, residual, cot, weights, vectors)


def hidden_body(
    layout,
    place,
    h_ref,
    e0,
    e1,
    e2,
    e3,
    x_ref,
    ma,
    ta,
    mb,
    tb,
    c1_ref,
    c2_ref,
    e_ref,
    out_ref,
    dh_ref,
    ga,
    fa,
    gb,
    fb,
    dc1_ref,
    h_t,
    e_t,
    total,
    up_ref,
    down_ref,
    grad_ref,
):
    step = pl.program_id(0)

    @pl.when(step == 0)
    def _():
        count = e0.shape[0]
        for j, ref in enumerate((e0, e1, e2, e3)):
            rows = slice(j * count, (j + 1) * count)
            e_ref[rows, :] = ref[...]
            e_t[:, rows] = ref[...].T
        h_t[...] = h_ref[...].T
        total[...] = x_ref[...] + c2_ref[...]
        dh_ref[...] = jnp.zeros_like(dh_ref)

    layout.join(place, True, ma, ta, 0, up_ref)
    layout.join(place, False, mb, tb, 0, down_ref)
    up = up_ref[...].astype(bf16)
    down = down_ref[...].astype(bf16)
    pre_act = dot(h_ref[...], up, 1, 0) + c1_ref[0]
    half = 0.5 * (1.0 + lax.erf(pre_act * root_half))
    hidden = (pre_act * half).astype(bf16)
    slope = half + pre_act * jnp.exp(-0.5 * pre_act * pre_act) * inv_root_tau
    total[...] += dot(hidden, down, 1, 1)
    dpre = dot(e_ref[...], down, 1, 0) * slope
    dc1_ref[0] = jnp.sum(dpre, 0, keepdims=True)
    dpre_low = dpre.astype(bf16)
    grad_ref[...] = dot(e_t[...], hidden, 1, 0).astype(grad_ref.dtype)
    layout.cut(place, False, grad_ref, gb, fb, 0)
    grad_ref[...] = dot(h_t[...], dpre_low, 1, 0).astype(grad_ref.dtype)
    layout.cut(place, True, grad_ref, ga, fa, 0)
    dh_ref[...] += dot(dpre_low, up, 1, 1)

    @pl.when(step == pl.num_programs(0) - 1)
    def _():
        out_ref[...] = total[...].astype(bf16)


def hidden_both(layout, place, h_low, e_pieces, residual, pieces, c1_rows, c2_row):
    rows, width = h_low.shape
    count, blocks, block_rows, units = pieces[0].shape
    frames = whole(rows, width)
    piece = pl.BlockSpec((count, 1, block_rows, units), lambda i, s: (0, i, 0, 0))
    bias = pl.BlockSpec((1, 1, units), lambda i, s: (s[3] ^ i, 0, 0))
    return call(
        lambda *refs: hidden_body(layout, *refs),
        (blocks,),
        [frames]
        + [whole(*each.shape) for each in e_pieces]
        + [frames]
        + [piece] * 4
        + [bias, whole(1, width)],
        [frames, frames, frames] + [piece] * 4 + [bias],
        [
            jax.ShapeDtypeStruct((rows, width), bf16),
            jax.ShapeDtypeStruct((rows, width), bf16),
            jax.ShapeDtypeStruct((rows, width), f32),
        ]
        + [jax.ShapeDtypeStruct(pieces[0].shape, bf16)] * 4
        + [jax.ShapeDtypeStruct((blocks, 1, units), f32)],
        [
            pltpu.VMEM((width, rows), bf16),
            pltpu.VMEM((width, rows), bf16),
            pltpu.VMEM((rows, width), f32),
            layout.scratch(units),
            layout.scratch(units),
            layout.scratch(units),
        ],
        12 * rows * width * units * blocks,
        2 * rows * units * blocks,
        8 * width * units * blocks + 14 * rows * width,
        46,
    )(place, h_low, *e_pieces, residual, *pieces, c1_rows[:, None, :], c2_row[None])


def weigh_body(
    layout, place, h_ref, dq_ref, dkeep_ref, din_ref, dx_ref, o_ref, d_ref, ga, fa, gb, fb, grad_ref
):
    h_t = h_ref[...].T
    for plane in range(4):
        if plane == 0:
            d_ref[0] = dq_ref[...]
        elif plane < 3:
            part = dkeep_ref[plane - 1] + din_ref[plane - 1].astype(f32)
            d_ref[plane] = part.astype(bf16)
        if plane < 3:
            grad = dot(h_t, d_ref[plane], 1, 0)
        else:
            grad = dot(dx_ref[...].T, o_ref[...], 1, 0)
        grad_ref[...] = grad.astype(grad_ref.dtype)
        first = plane < 2
        layout.cut(place, first, grad_ref, ga if first else gb, fa if first else fb, plane % 2)


def weigh(layout, place, h_low, dquery, dkeep, din, dx_low, context):
    rows, width = h_low.shape
    frames = whole(rows, width)
    shape = (layout.count, 2, layout.rows, width)
    return call(
        lambda *refs: weigh_body(layout, *refs),
        (1,),
        [frames, frames, whole(2, rows, width), whole(2, rows, width), frames, frames],
        [whole(3, rows, width)] + [whole(*shape)] * 4,
        [jax.ShapeDtypeStruct((3, rows, width), bf16)] + [jax.ShapeDtypeStruct(shape, bf16)] * 4,
        [layout.scratch(width)],
        8 * rows * width * width,
        0,
        8 * width * width + 28 * rows * width,
        36,
    )(place, h_low, dquery, dkeep, din, dx_low, context)


def finish_body(place, d_ref, w_ref, x_ref, dx_ref, vec_ref, out_ref, sums_ref):
    dnorm = None
    for plane in range(3):
        dnorm = add_dot(dnorm, d_ref[plane], w_ref[plane], 1, 1)
    _, normed, inv_scale = layer_norm(x_ref[...].astype(f32), vec_ref[0:1, :], vec_ref[1:2, :])
    out = dx_ref[...] + norm_back(dnorm, normed, inv_scale, vec_ref[0:1, :])
    out_ref[...] = out.astype(bf16)
    gather_sums(sums_ref, dnorm * normed, dnorm)


def finish(place, dproj, weights, x_low, dresidual, vectors):
    rows, width = x_low.shape
    return call(
        finish_body,
        (rows // TILE,),
        [
            tiles(width, 3),
            whole(3, width, width),
            tiles(width),
            tiles(width),
            whole(*vectors.shape),
        ],
        [tiles(width), whole(2, width)],
        [jax.ShapeDtypeStruct((rows, width), bf16), jax.ShapeDtypeStruct((2, width), f32)],
        [],
        6 * rows * width * width,
        0,
        6 * width * width + 14 * rows * width,
        28,
    )(place, dproj, weights, x_low, dresidual, vectors)


def update(refs, gradient):
    out = (gradient,) + adamw(refs[0][...], gradient, refs[1][...], refs[2][...], decay_rate)
    for ref, values in zip(refs[3:], out):
        ref[...] = values


def update_ff_body(place, *refs):
    terms, refs = refs[:-14], refs[-14:]
    total = sum(term[...].astype(f32) for term in terms)
    update(refs[0:3] + refs[6:10], total[0, 0])
    update(refs[3:6] + refs[10:14], total[1, 0])


def update_proj_body(place, *refs):
    terms, refs = refs[:-14], refs[-14:]
    total = sum(term[...].astype(f32) for term in terms)
    update(refs[0:3] + refs[6:10], total[:3])
    update(refs[3:6] + refs[10:14], total[3].T)


def update_both(place, body, terms, first, second):
    shapes = [first[0].shape] * 4 + [second[0].shape] * 4
    inputs = list(terms) + list(first) + list(second)
    out = call(
        body,
        (1,),
        [whole(*each.shape) for each in inputs],
        [whole(*shape) for shape in shapes],
        [jax.ShapeDtypeStruct(shape, f32) for shape in shapes],
        [],
        0,
        first[0].size + second[0].size,
        32 * (first[0].size + second[0].size),
        20,
    )(place, *inputs)
    return out[:4], out[4:]


def bits(count):
    step = 1
    while step < count:
        yield step
        step *= 2


class Grid:
    def __init__(self):
        self.fsdp = lax.axis_size("fsdp")
        self.outer = self.fsdp // CORES
        self.ctx = lax.axis_size("ctx")
        self.tensor = lax.axis_size("tensor")
        here = lax.axis_index(AXES)
        self.place = lax.rem(
            here // jnp.array([CORES * self.ctx * self.tensor, self.ctx * self.tensor, self.tensor, 1]),
            jnp.array([self.outer, CORES, self.ctx, self.tensor]),
        ).astype(jnp.int32)
        self.z = lax.axis_index("tensor")

    def index(self, fo, core, y, z):
        return ((fo * CORES + core) * self.ctx + y) * self.tensor + z

    def move(self, data, target):
        pairs = []
        for fo in range(self.outer):
            for core in range(CORES):
                for y in range(self.ctx):
                    for z in range(self.tensor):
                        pairs.append((self.index(fo, core, y, z), self.index(*target(fo, core, y, z))))
        return lax.ppermute(data, AXES, pairs)

    def swap(self, data, axis, bit=1):
        dim = ("x", "core", "y", "z").index(axis)
        return self.move(data, lambda *at: tuple(v ^ bit if i == dim else v for i, v in enumerate(at)))

    def turn(self, rows):
        for bit in bits(self.tensor):
            order = [j ^ bit for j in range(self.tensor)]
            other = jnp.stack([rows[j] for j in order])
            rows = jnp.where((self.z & bit) != 0, other, rows)
        return rows


def over_tensor(grid, shard):
    data = shard[None]
    for bit in bits(grid.tensor):
        data = jnp.concatenate([data, grid.swap(data, "z", bit)], 0)
    return data


def axis_bits(grid, ctx_first):
    outer = [("x", bit) for bit in bits(grid.outer)]
    inner = [("y", bit) for bit in bits(grid.ctx)]
    return inner + outer if ctx_first else outer + inner


def spread(grid, planes, ctx_first):
    data = planes[None]
    for axis, bit in axis_bits(grid, ctx_first):
        data = jnp.concatenate([data, grid.swap(data, axis, bit)], 0)
    return data, grid.swap(data, "core")


def collect(grid, keep, give, ctx_first):
    terms = [keep, grid.swap(give, "core")]
    for axis, bit in reversed(axis_bits(grid, ctx_first)):
        half = terms[0].shape[0] // 2
        out = sum(term[half:].astype(f32) for term in terms).astype(bf16)
        terms = [term[:half] for term in terms] + [grid.swap(out, axis, bit)]
    return [term[0] for term in terms]


def total_of(terms):
    return sum(term.astype(f32) for term in terms)


def to_owner(grid, terms, split):
    for bit in reversed(list(bits(grid.tensor))):
        halves = [split(term, bit) for term in terms]
        out = total_of([half[1] for half in halves]).astype(bf16)
        terms = [half[0] for half in halves] + [grid.swap(out, "z", bit)]
    return terms


def sum_everywhere(grid, rows):
    rows = rows + grid.swap(rows, "core")
    for axis, count in (("x", grid.outer), ("y", grid.ctx), ("z", grid.tensor)):
        for bit in bits(count):
            rows = rows + grid.swap(rows, axis, bit)
    return rows


def clips_in(grid, frames):
    pieces = []
    for j in range(grid.tensor):
        out = lax.dynamic_index_in_dim(frames, grid.z ^ j, 0, False)
        pieces.append(grid.move(out, lambda f, c, y, z: (f, y, c, z ^ j)))
    return pieces


def clips_out_body(place, *refs):
    out_ref = refs[-1]
    for j, ref in enumerate(refs[:-1]):
        out_ref[pl.ds(place[3] ^ j, 1)] = ref[...].astype(out_ref.dtype)[None]


def clips_out(grid, rows, kind):
    step = rows.shape[0] // grid.tensor
    pieces = []
    for j in range(grid.tensor):
        out = rows[j * step : (j + 1) * step]
        pieces.append(grid.move(out, lambda f, c, y, z: (f, y, c, z ^ j)))
    shape = (step, rows.shape[1])
    return call(
        clips_out_body,
        (1,),
        [whole(*shape)] * grid.tensor,
        whole(grid.tensor, *shape),
        jax.ShapeDtypeStruct((grid.tensor,) + shape, kind),
        [],
        0,
        0,
        8 * rows.size,
        10,
    )(grid.place, *pieces)


def step_of(
    frames_in,
    out_cotangent,
    attend_weight,
    output_weight,
    up_weight,
    down_weight,
    vectors,
    attend_mean,
    attend_square,
    output_mean,
    output_square,
    up_mean,
    up_square,
    down_mean,
    down_square,
    vector_mean,
    vector_square,
):
    grid = Grid()
    place = grid.place
    width = frames_in.shape[2]
    part = attend_weight.shape[2]
    layout = Layout(grid.outer, grid.ctx, up_weight.shape[0])

    shard = jnp.concatenate([attend_weight.astype(bf16), output_weight.astype(bf16).T[None]], 0)
    proj = over_tensor(grid, shard)
    proj = jnp.concatenate([proj[j] for j in range(grid.tensor)], 2)
    x_pieces = clips_in(grid, frames_in)
    proj_pieces = spread(grid, proj[:2], True) + spread(grid, proj[2:], False)
    shard = jnp.stack([up_weight.astype(bf16), down_weight.astype(bf16).T])
    ff = over_tensor(grid, shard)
    ff_pieces = spread(grid, ff[:, 0], True) + spread(grid, ff[:, 1], False)
    e_pieces = clips_in(grid, out_cotangent)

    def turned(row):
        return grid.turn(row.reshape(grid.tensor, part)).reshape(1, width)

    biases = jnp.concatenate([turned(vectors[2]), turned(vectors[3])], 0)

    x_low, in_norm1, queries, own, weights = project(
        layout, place, x_pieces, proj_pieces, vectors, biases
    )
    far = grid.swap(own, "core")
    context, log_total = attend_forward(place, queries, own, far)
    residual, in_norm2 = mix(place, x_low, context, weights, vectors)
    cot_low, result, dnorm2, ga, fa, gb, fb, grad_c1 = hidden_both(
        layout, place, in_norm2, e_pieces, residual, ff_pieces, vectors[8:12], vectors[7]
    )
    frames_out = clips_out(grid, result, bf16)
    ff_a = collect(grid, ga, fa, True)
    ff_b = collect(grid, gb, fb, False)

    dresidual, dres_low, dcontext, mid_sums = unmix(
        place, dnorm2, residual, cot_low, weights, vectors
    )
    dquery, dkeep, dgive, sums = attend_backward(
        place, queries, own, far, context, dcontext, log_total
    )
    din = grid.swap(dgive, "core")
    dproj, ga, fa, gb, fb = weigh(layout, place, in_norm1, dquery, dkeep, din, dres_low, context)
    proj_a = collect(grid, ga, fa, True)
    proj_b = collect(grid, gb, fb, False)
    dinputs, end_sums = finish(place, dproj, weights, x_low, dresidual, vectors)
    frames_grad = clips_out(grid, dinputs, f32)

    vector_part = jnp.concatenate(
        [end_sums, jnp.stack([turned(sums[0])[0], turned(sums[1])[0]]), mid_sums, grad_c1[:, 0, :]],
        0,
    )
    vector_grad = sum_everywhere(grid, vector_part)

    def by_block(term, bit):
        return term[:, :bit], term[:, bit:]

    def by_column(term, bit):
        return term[..., : bit * part], term[..., bit * part :]

    terms = to_owner(grid, [jnp.stack(pair) for pair in zip(ff_a, ff_b)], by_block)
    ups, downs = update_both(
        place,
        update_ff_body,
        terms,
        (up_weight, up_mean, up_square),
        (down_weight.T, down_mean.T, down_square.T),
    )
    up_grad, up_new, up_mean_new, up_square_new = ups
    down_grad, down_new, down_mean_new, down_square_new = [each.T for each in downs]
    terms = to_owner(grid, [jnp.concatenate(pair, 0) for pair in zip(proj_a, proj_b)], by_column)
    attends, outputs = update_both(
        place,
        update_proj_body,
        terms,
        (attend_weight, attend_mean, attend_square),
        (output_weight, output_mean, output_square),
    )
    attend_grad, attend_new, attend_mean_new, attend_square_new = attends
    output_grad, output_new, output_mean_new, output_square_new = outputs
    vector_new, vector_mean_new, vector_square_new = adamw(
        vectors, vector_grad, vector_mean, vector_square, 0.0
    )
    return (
        frames_out,
        frames_grad,
        attend_grad,
        output_grad,
        up_grad,
        down_grad,
        vector_grad,
        attend_new,
        output_new,
        up_new,
        down_new,
        vector_new,
        attend_mean_new,
        attend_square_new,
        output_mean_new,
        output_square_new,
        up_mean_new,
        up_square_new,
        down_mean_new,
        down_square_new,
        vector_mean_new,
        vector_square_new,
    )


def solution(mesh):
    frames = P("fsdp", ("ctx", "tensor"), None)
    attend = P(None, ("fsdp", "ctx"), "tensor")
    tall = P("tensor", ("fsdp", "ctx"))
    flat = P(("fsdp", "ctx"), "tensor")
    weights = (attend, tall, flat, tall)
    return jax.shard_map(
        step_of,
        mesh=mesh,
        in_specs=(frames, frames)
        + weights
        + (P(), attend, attend, tall, tall, flat, flat, tall, tall, P(), P()),
        out_specs=(frames, frames)
        + weights
        + (P(),)
        + weights
        + (P(), attend, attend, tall, tall, flat, flat, tall, tall, P(), P()),
        check_vma=False,
    )
```

```python
import jax
import jax.numpy as jnp
from jax import lax
from jax.experimental import pallas as pl
from jax.experimental.pallas import tpu as pltpu
from jax.sharding import PartitionSpec as P


HD = 64
STEP = 3
CORES = 2

norm_eps = 1e-05
learn_rate = 0.04
beta_one = 0.9
beta_two = 0.999
adam_eps = 1e-08
decay_rate = 0.01
root_half = 0.7071067811865476
inv_root_tau = 0.3989422804014327

AXES = ("fsdp", "ctx", "tensor")
f32 = jnp.float32
bf16 = jnp.bfloat16


def layer_norm(inputs, gain_row, shift_row):
    row_mean = jnp.mean(inputs, -1, keepdims=True)
    centred = inputs - row_mean
    variance = jnp.mean(centred * centred, -1, keepdims=True)
    inv_scale = lax.rsqrt(variance + norm_eps)
    normed = centred * inv_scale
    return (normed * gain_row + shift_row, normed, inv_scale)


def norm_back(upstream, normed, inv_scale, gain_row):
    dnormed = upstream * gain_row
    mean_one = jnp.mean(dnormed, -1, keepdims=True)
    mean_two = jnp.mean(dnormed * normed, -1, keepdims=True)
    return inv_scale * (dnormed - mean_one - normed * mean_two)


def adamw(weight_now, gradient, mean_old, square_old, decay):
    mean_new = beta_one * mean_old + (1.0 - beta_one) * gradient
    square_new = beta_two * square_old + (1.0 - beta_two) * gradient * gradient
    mean_hat = mean_new / (1.0 - beta_one**STEP)
    square_hat = square_new / (1.0 - beta_two**STEP)
    weight_new = weight_now - learn_rate * (
        mean_hat / (jnp.sqrt(square_hat) + adam_eps) + decay * weight_now
    )
    return (weight_new, mean_new, square_new)


def dot(a, b, ca, cb):
    return lax.dot_general(a, b, (((ca,), (cb,)), ((), ())), preferred_element_type=f32)


def add_dot(total, a, b, ca, cb):
    part = dot(a, b, ca, cb)
    return part if total is None else total + part


class Layout:
    def __init__(self, outer, ctx, rows):
        self.outer, self.ctx, self.rows = outer, ctx, rows
        self.count = outer * ctx
        self.total = self.count * CORES * rows

    def offset(self, place, ctx_first, other, j):
        if ctx_first:
            jy, jf = j % self.ctx, j // self.ctx
        else:
            jf, jy = j % self.outer, j // self.outer
        block = ((place[0] ^ jf) * CORES + (place[1] ^ other)) * self.ctx + (place[2] ^ jy)
        return pl.multiple_of(block * self.rows, self.rows)

    def scratch(self, width):
        kind = bf16 if self.rows % 16 == 0 else f32
        return pltpu.VMEM((self.total, width), kind)

    def blocks(self, place, ctx_first, refs):
        half = self.count // 2
        for other in range(CORES):
            for j in range(self.count):
                rows = pl.ds(self.offset(place, ctx_first, other, j), self.rows)
                yield rows, refs[2 * other + j // half], j % half

    def join(self, place, ctx_first, refs, plane, target):
        for rows, ref, j in self.blocks(place, ctx_first, refs):
            target[rows, :] = ref[j, plane].astype(target.dtype)

    def cut(self, place, ctx_first, source, refs, plane):
        for rows, ref, j in self.blocks(place, ctx_first, refs):
            ref[j, plane] = source[rows, :].astype(bf16)


def mirror(j, count):
    out, step = 0, 1
    while step < count:
        out = out * 2 + (j // step) % 2
        step *= 2
    return out


def turn_row(z, row, count, back=False):
    size = row.shape[1] // count
    blocks = [row[:, j * size : (j + 1) * size] for j in range(count)]
    out = row
    for at in range(count):
        source = [mirror(j ^ at, count) if back else at ^ mirror(j, count) for j in range(count)]
        out = jnp.where(z == at, jnp.concatenate([blocks[j] for j in source], 1), out)
    return out


def whole(*shape):
    return pl.BlockSpec(shape, lambda i, s: (0,) * len(shape))


IN_HBM = {
    "hidden_both": range(1, 12),
    "attend_backward": range(7),
    "weigh": (0, 4, 5),
    "finish": (1, 2, 3),
    "update_ff": range(-6, 0),
    "update_proj": range(-6, 0),
}


def call(body, name, grid, in_specs, out_specs, out_shape, scratch, flops, trans, moved, mib):
    kernel = pl.pallas_call(
        body,
        grid_spec=pltpu.PrefetchScalarGridSpec(
            num_scalar_prefetch=1,
            grid=grid,
            in_specs=in_specs,
            out_specs=out_specs,
            scratch_shapes=scratch,
        ),
        out_shape=out_shape,
        compiler_params=pltpu.CompilerParams(vmem_limit_bytes=mib * 1024 * 1024),
        cost_estimate=pl.CostEstimate(flops=flops, transcendentals=trans, bytes_accessed=moved),
    )

    def run(place, *arrays):
        stay = IN_HBM.get(name, ())
        stay = [j % len(arrays) for j in stay]
        arrays = [
            pltpu.with_memory_space_constraint(each, pltpu.HBM) if j in stay else each
            for j, each in enumerate(arrays)
        ]
        return kernel(place, *arrays)

    return run


def project_body(
    layout, tensor, place, x_ref, *refs
):
    sets = refs[0:4], refs[4:8]
    vec_ref, h_ref, q_ref, kv_ref, w_ref, joined = refs[8:]
    bias_query = turn_row(place[3], vec_ref[2:3, :], tensor)
    bias_value = turn_row(place[3], vec_ref[3:4, :], tensor)
    norm_out, _, _ = layer_norm(x_ref[...].astype(f32), vec_ref[0:1, :], vec_ref[1:2, :])
    h_ref[...] = norm_out.astype(bf16)
    for plane in range(4):
        first = plane < 2
        layout.join(place, first, sets[plane // 2], plane % 2, joined)
        weight = joined[...].astype(bf16)
        w_ref[plane] = weight
        if plane == 3:
            break
        out = dot(h_ref[...], weight, 1, 0)
        if plane == 0:
            q_ref[...] = (out + bias_query).astype(bf16)
        elif plane == 1:
            kv_ref[0] = out.astype(bf16)
        else:
            kv_ref[1] = (out + bias_value).astype(bf16)


def project(layout, tensor, place, x_low, pieces, vectors):
    rows, width = x_low.shape
    frames = whole(rows, width)
    return call(
        lambda *refs: project_body(layout, tensor, *refs),
        "project",
        (1,),
        [frames]
        + [whole(*pieces[0].shape)] * 8
        + [whole(*vectors.shape)],
        [frames, frames, whole(2, rows, width), whole(4, width, width)],
        [jax.ShapeDtypeStruct((rows, width), bf16)] * 2
        + [
            jax.ShapeDtypeStruct((2, rows, width), bf16),
            jax.ShapeDtypeStruct((4, width, width), bf16),
        ],
        [layout.scratch(width)],
        6 * rows * width * width,
        0,
        16 * width * width + 10 * rows * width,
        32,
    )(place, x_low, *pieces, vectors)


def attend_forward_body(place, q_ref, own_ref, far_ref, o_ref, lse_ref):
    lane = lax.broadcasted_iota(jnp.int32, (1, 2 * HD), 1)
    queries = q_ref[...]
    val_t = (own_ref[1].T, far_ref[1].T)
    parts = []
    for head in range(2):
        mask = ((lane // HD) == head).astype(f32) * HD ** (-0.5)
        q_head = queries * mask.astype(bf16)
        s_a = dot(own_ref[0], q_head, 1, 1)
        s_b = dot(far_ref[0], q_head, 1, 1)
        top = jnp.maximum(
            jnp.max(s_a, 0, keepdims=True), jnp.max(s_b, 0, keepdims=True)
        )
        e_a = jnp.exp(s_a - top)
        e_b = jnp.exp(s_b - top)
        total = jnp.sum(e_a, 0, keepdims=True) + jnp.sum(e_b, 0, keepdims=True)
        lse_ref[0, head : head + 1, :] = top + jnp.log(total)
        inv = 1.0 / total
        rows = slice(head * HD, (head + 1) * HD)
        parts.append(
            dot(val_t[0][rows], (e_a * inv).astype(bf16), 1, 0)
            + dot(val_t[1][rows], (e_b * inv).astype(bf16), 1, 0)
        )
    o_ref[...] = jnp.concatenate(parts, 0).T.astype(bf16)


def attend_forward(place, queries, own, far):
    rows, width = queries.shape
    pairs = width // (2 * HD)
    block = pl.BlockSpec((rows, 2 * HD), lambda i, s: (0, i))
    both = pl.BlockSpec((2, rows, 2 * HD), lambda i, s: (0, 0, i))
    return call(
        attend_forward_body,
        "attend_forward",
        (pairs,),
        [block, both, both],
        [block, pl.BlockSpec((1, 2, rows), lambda i, s: (i, 0, 0))],
        [
            jax.ShapeDtypeStruct((rows, width), bf16),
            jax.ShapeDtypeStruct((pairs, 2, rows), f32),
        ],
        [],
        8 * rows * rows * width,
        2 * rows * rows * width // HD,
        12 * rows * width,
        24,
    )(place, queries, own, far)


def attend_backward_body(
    place,
    q_ref,
    own_ref,
    far_ref,
    o_ref,
    do_ref,
    lse_ref,
    dq_ref,
    dkeep_ref,
    dgive_ref,
    sums_ref,
):
    lane = lax.broadcasted_iota(jnp.int32, (1, 2 * HD), 1)
    queries = q_ref[...]
    dcontext = do_ref[...]
    weighed = (dcontext.astype(f32) * o_ref[...].astype(f32)).T
    key_t = (own_ref[0].T, far_ref[0].T)
    dkeys = [None, None]
    dvals = [None, None]
    dq_parts = []
    for head in range(2):
        mask = ((lane // HD) == head).astype(f32)
        q_head = queries * (mask * HD ** (-0.5)).astype(bf16)
        do_head = dcontext * mask.astype(bf16)
        rows = slice(head * HD, (head + 1) * HD)
        delta = jnp.sum(weighed[rows], 0, keepdims=True)
        lse = lse_ref[0, head : head + 1, :]
        dq_head = None
        for part, ref in enumerate((own_ref, far_ref)):
            probs = jnp.exp(dot(ref[0], q_head, 1, 1) - lse)
            dprobs = dot(ref[1], do_head, 1, 1)
            dscores = (probs * (dprobs - delta)).astype(bf16)
            dvals[part] = add_dot(dvals[part], probs.astype(bf16), do_head, 1, 0)
            dkeys[part] = add_dot(dkeys[part], dscores, q_head, 1, 0)
            dq_head = add_dot(dq_head, key_t[part][rows], dscores, 1, 0)
        dq_parts.append(dq_head)
    dquery = jnp.concatenate(dq_parts, 0).T * HD ** (-0.5)
    dq_ref[...] = dquery.astype(bf16)
    dkeep_ref[0] = dkeys[0]
    dkeep_ref[1] = dvals[0]
    dgive_ref[0] = dkeys[1].astype(bf16)
    dgive_ref[1] = dvals[1].astype(bf16)
    sums_ref[0:1, :] = jnp.sum(dquery, 0, keepdims=True)
    sums_ref[1:2, :] = jnp.sum(dvals[0], 0, keepdims=True) + jnp.sum(dvals[1], 0, keepdims=True)


def attend_backward(place, queries, own, far, context, dcontext, lse):
    rows, width = queries.shape
    pairs = width // (2 * HD)
    block = pl.BlockSpec((rows, 2 * HD), lambda i, s: (0, i))
    both = pl.BlockSpec((2, rows, 2 * HD), lambda i, s: (0, 0, i))
    return call(
        attend_backward_body,
        "attend_backward",
        (pairs,),
        [block, both, both, block, block, pl.BlockSpec((1, 2, rows), lambda i, s: (i, 0, 0))],
        [block, both, both, pl.BlockSpec((2, 2 * HD), lambda i, s: (0, i))],
        [
            jax.ShapeDtypeStruct((rows, width), bf16),
            jax.ShapeDtypeStruct((2, rows, width), f32),
            jax.ShapeDtypeStruct((2, rows, width), bf16),
            jax.ShapeDtypeStruct((2, width), f32),
        ],
        [],
        20 * rows * rows * width,
        2 * rows * rows * width // HD,
        32 * rows * width,
        32,
    )(place, queries, own, far, context, dcontext, lse)


TILE = 512


def tiles(width, *lead):
    return pl.BlockSpec(lead + (TILE, width), lambda i, s: (0,) * len(lead) + (i, 0))


def gather_sums(sums_ref, *rows):
    @pl.when(pl.program_id(0) == 0)
    def _():
        sums_ref[...] = jnp.zeros_like(sums_ref)

    for j, values in enumerate(rows):
        sums_ref[j : j + 1, :] += jnp.sum(values, 0, keepdims=True)


def mix_body(place, x_ref, o_ref, w_ref, vec_ref, x1_ref, h_ref):
    residual = x_ref[...].astype(f32) + dot(o_ref[...], w_ref[0], 1, 1) + vec_ref[4:5, :]
    x1_ref[...] = residual
    norm_out, _, _ = layer_norm(residual, vec_ref[5:6, :], vec_ref[6:7, :])
    h_ref[...] = norm_out.astype(bf16)


def mix(place, x_low, context, weights, vectors):
    rows, width = x_low.shape
    return call(
        mix_body,
        "mix",
        (rows // TILE,),
        [
            tiles(width),
            tiles(width),
            pl.BlockSpec((1, width, width), lambda i, s: (3, 0, 0)),
            whole(*vectors.shape),
        ],
        [tiles(width), tiles(width)],
        [jax.ShapeDtypeStruct((rows, width), f32), jax.ShapeDtypeStruct((rows, width), bf16)],
        [],
        2 * rows * width * width,
        0,
        2 * width * width + 10 * rows * width,
        20,
    )(place, x_low, context, weights, vectors)


def unmix_body(place, dh_ref, x1_ref, e_ref, w_ref, vec_ref, dx_ref, low_ref, do_ref, sums_ref):
    cot = e_ref[...].astype(f32)
    dnorm = dh_ref[...]
    _, normed, inv_scale = layer_norm(x1_ref[...], vec_ref[5:6, :], vec_ref[6:7, :])
    dresidual = cot + norm_back(dnorm, normed, inv_scale, vec_ref[5:6, :])
    dx_ref[...] = dresidual
    low = dresidual.astype(bf16)
    low_ref[...] = low
    do_ref[...] = dot(low, w_ref[0], 1, 0).astype(bf16)
    gather_sums(sums_ref, dresidual, dnorm * normed, dnorm, cot)


def unmix(place, dnorm, residual, cot, weights, vectors):
    rows, width = residual.shape
    return call(
        unmix_body,
        "unmix",
        (rows // TILE,),
        [
            tiles(width),
            tiles(width),
            tiles(width),
            pl.BlockSpec((1, width, width), lambda i, s: (3, 0, 0)),
            whole(*vectors.shape),
        ],
        [tiles(width), tiles(width), tiles(width), whole(4, width)],
        [
            jax.ShapeDtypeStruct((rows, width), f32),
            jax.ShapeDtypeStruct((rows, width), bf16),
            jax.ShapeDtypeStruct((rows, width), bf16),
            jax.ShapeDtypeStruct((4, width), f32),
        ],
        [],
        2 * rows * width * width,
        0,
        2 * width * width + 18 * rows * width,
        24,
    )(place, dnorm, residual, cot, weights, vectors)


def hidden_body(
    layout,
    place,
    h_ref,
    e_ref,
    x_ref,
    *refs,
):
    up_in, down_in = refs[0:4], refs[4:8]
    c1_ref, c2_ref = refs[8:10]
    out_ref, dh_ref = refs[10:12]
    up_out, down_out = refs[12:16], refs[16:20]
    dc1_ref, h_t, e_t, total, up_ref, down_ref, grad_ref = refs[20:]
    step = pl.program_id(0)

    @pl.when(step == 0)
    def _():
        e_t[...] = e_ref[...].T
        h_t[...] = h_ref[...].T
        total[...] = x_ref[...] + c2_ref[...]
        dh_ref[...] = jnp.zeros_like(dh_ref)

    layout.join(place, True, up_in, 0, up_ref)
    layout.join(place, False, down_in, 0, down_ref)
    up = up_ref[...].astype(bf16)
    down = down_ref[...].astype(bf16)
    pre_act = dot(h_ref[...], up, 1, 0) + c1_ref[0]
    half = 0.5 * (1.0 + lax.erf(pre_act * root_half))
    hidden = (pre_act * half).astype(bf16)
    slope = half + pre_act * jnp.exp(-0.5 * pre_act * pre_act) * inv_root_tau
    total[...] += dot(hidden, down, 1, 1)
    dpre = dot(e_ref[...], down, 1, 0) * slope
    dc1_ref[0] = jnp.sum(dpre, 0, keepdims=True)
    dpre_low = dpre.astype(bf16)
    grad_ref[...] = dot(e_t[...], hidden, 1, 0).astype(grad_ref.dtype)
    layout.cut(place, False, grad_ref, down_out, 0)
    grad_ref[...] = dot(h_t[...], dpre_low, 1, 0).astype(grad_ref.dtype)
    layout.cut(place, True, grad_ref, up_out, 0)
    dh_ref[...] += dot(dpre_low, up, 1, 1)

    @pl.when(step == pl.num_programs(0) - 1)
    def _():
        out_ref[...] = total[...].astype(bf16)


def hidden_both(layout, place, h_low, cot, residual, pieces, c1_rows, c2_row):
    rows, width = h_low.shape
    count, blocks, block_rows, units = pieces[0].shape
    frames = whole(rows, width)
    piece = pl.BlockSpec((count, 1, block_rows, units), lambda i, s: (0, i, 0, 0))
    bias = pl.BlockSpec((1, 1, units), lambda i, s: (s[3] ^ mirror(i, blocks), 0, 0))
    return call(
        lambda *refs: hidden_body(layout, *refs),
        "hidden_both",
        (blocks,),
        [frames, frames, frames]
        + [piece] * 8
        + [bias, whole(1, width)],
        [frames, frames]
        + [piece] * 8
        + [bias],
        [jax.ShapeDtypeStruct((rows, width), bf16), jax.ShapeDtypeStruct((rows, width), f32)]
        + [jax.ShapeDtypeStruct(pieces[0].shape, bf16)] * 8
        + [jax.ShapeDtypeStruct((blocks, 1, units), f32)],
        [
            pltpu.VMEM((width, rows), bf16),
            pltpu.VMEM((width, rows), bf16),
            pltpu.VMEM((rows, width), f32),
            layout.scratch(units),
            layout.scratch(units),
            layout.scratch(units),
        ],
        12 * rows * width * units * blocks,
        2 * rows * units * blocks,
        8 * width * units * blocks + 14 * rows * width,
        46,
    )(place, h_low, cot, residual, *pieces, c1_rows[:, None, :], c2_row[None])


def weigh_body(
    layout, place, h_ref, dq_ref, dkeep_ref, din_ref, dx_ref, o_ref, d_ref, *refs
):
    sets, grad_ref = (refs[0:4], refs[4:8]), refs[8]
    h_t = h_ref[...].T
    for plane in range(4):
        if plane == 0:
            d_ref[0] = dq_ref[...]
        elif plane < 3:
            part = dkeep_ref[plane - 1] + din_ref[plane - 1].astype(f32)
            d_ref[plane] = part.astype(bf16)
        if plane < 3:
            grad = dot(h_t, d_ref[plane], 1, 0)
        else:
            grad = dot(dx_ref[...].T, o_ref[...], 1, 0)
        grad_ref[...] = grad.astype(grad_ref.dtype)
        layout.cut(place, plane < 2, grad_ref, sets[plane // 2], plane % 2)


def weigh(layout, place, h_low, dquery, dkeep, din, dx_low, context):
    rows, width = h_low.shape
    frames = whole(rows, width)
    shape = (layout.count // 2, 2, layout.rows, width)
    return call(
        lambda *refs: weigh_body(layout, *refs),
        "weigh",
        (1,),
        [frames, frames, whole(2, rows, width), whole(2, rows, width), frames, frames],
        [whole(3, rows, width)] + [whole(*shape)] * 8,
        [jax.ShapeDtypeStruct((3, rows, width), bf16)] + [jax.ShapeDtypeStruct(shape, bf16)] * 8,
        [layout.scratch(width)],
        8 * rows * width * width,
        0,
        8 * width * width + 28 * rows * width,
        36,
    )(place, h_low, dquery, dkeep, din, dx_low, context)


def finish_body(tensor, place, d_ref, w_ref, x_ref, dx_ref, vec_ref, mid_ref, qv_ref, dc1_ref, *refs):
    out_ref, sums_ref = refs
    dnorm = None
    for plane in range(3):
        dnorm = add_dot(dnorm, d_ref[plane], w_ref[plane], 1, 1)
    _, normed, inv_scale = layer_norm(x_ref[...].astype(f32), vec_ref[0:1, :], vec_ref[1:2, :])
    out = dx_ref[...] + norm_back(dnorm, normed, inv_scale, vec_ref[0:1, :])
    out_ref[...] = out.astype(bf16)
    sums_ref[0:1, :] = jnp.sum(dnorm * normed, 0, keepdims=True)
    sums_ref[1:2, :] = jnp.sum(dnorm, 0, keepdims=True)
    for j in range(2):
        sums_ref[2 + j : 3 + j, :] = turn_row(place[3], qv_ref[j : j + 1, :], tensor, True)
    sums_ref[4:8, :] = mid_ref[...]
    for j in range(dc1_ref.shape[0]):
        sums_ref[8 + j : 9 + j, :] = dc1_ref[j]


def finish(place, dproj, weights, x_low, dresidual, vectors, rows_in, tensor):
    rows, width = x_low.shape
    part = (rows, width)
    return call(
        lambda *refs: finish_body(tensor, *refs),
        "finish",
        (rows // TILE,),
        [
            tiles(width, 3),
            whole(3, width, width),
            tiles(width),
            tiles(width),
            whole(*vectors.shape),
        ]
        + [whole(*each.shape) for each in rows_in],
        [whole(*part), whole(*vectors.shape)],
        [jax.ShapeDtypeStruct(part, bf16)] + [jax.ShapeDtypeStruct(vectors.shape, f32)],
        [],
        6 * rows * width * width,
        0,
        6 * width * width + 14 * rows * width,
        28,
    )(place, dproj, weights, x_low, dresidual, vectors, *rows_in)


def update(refs, gradient):
    out = (gradient,) + adamw(refs[0][...], gradient, refs[1][...], refs[2][...], decay_rate)
    for ref, values in zip(refs[3:], out):
        ref[...] = values


def pick(ref, at):
    values = ref[...]
    return values.reshape(values.shape[len(at[0]) :])


def specs_of(terms):
    specs = []
    for array, lead, rows in terms:
        rest = array.shape[len(lead) :]
        if rows is None:
            index, block = 0, rest
        else:
            index, count = rows
            block = (count,) + rest[1:]
        shape = (1,) * len(lead) + block
        at = tuple(lead) + (index,) + (0,) * (len(block) - 1)
        specs.append(pl.BlockSpec(shape, lambda i, s, at=at: at))
    return specs


def merge(place, name, groups, columns=None):
    terms = [term for group in groups for term in group]
    shapes = []
    for group in groups:
        array, lead, rows = group[0]
        shape = array.shape[len(lead) :]
        shape = shape if rows is None else (rows[1],) + shape[1:]
        shapes.append(shape if columns is None else shape[:-1] + (columns.stop - columns.start,))
    stacked = columns is None
    out = (len(groups),) + shapes[0] if stacked else (sum(x[0] for x in shapes),) + shapes[0][1:]

    def body(place, *refs):
        out_ref, refs = refs[-1], list(refs[:-1])
        first = 0
        for g, group in enumerate(groups):
            total = None
            for _, lead, _ in group:
                values = pick(refs.pop(0), (lead, None)).astype(f32)
                if columns is not None and values.shape[-1] > shapes[g][-1]:
                    values = values[..., columns]
                total = values if total is None else total + values
            if stacked:
                out_ref[g] = total.astype(bf16)
            else:
                out_ref[first : first + shapes[g][0]] = total.astype(bf16)
            first += shapes[g][0]

    return call(
        body,
        name,
        (1,),
        specs_of(terms),
        whole(*out),
        jax.ShapeDtypeStruct(out, bf16),
        [],
        0,
        0,
        4 * len(terms) * shapes[0][-1] * shapes[0][-2],
        16,
    )(place, *[array for array, _, _ in terms])


def update_both(place, name, groups, columns, split, first, second):
    terms = [term for group in groups for term in group]
    shapes = [first[0].shape] * 4 + [second[0].shape] * 4
    states = list(first) + list(second)

    def body(place, *refs):
        refs = list(refs)
        sums = []
        for group in groups:
            total = None
            for _, lead, _ in group:
                values = pick(refs.pop(0), (lead, None)).astype(f32)
                if columns is not None and values.shape[-1] > columns:
                    values = values[..., :columns]
                total = values if total is None else total + values
            sums.append(total)
        grads = split(*sums)
        update(refs[0:3] + refs[6:10], grads[0])
        update(refs[3:6] + refs[10:14], grads[1])

    out = call(
        body,
        name,
        (1,),
        specs_of(terms) + [whole(*each.shape) for each in states],
        [whole(*shape) for shape in shapes],
        [jax.ShapeDtypeStruct(shape, f32) for shape in shapes],
        [],
        0,
        first[0].size + second[0].size,
        32 * (first[0].size + second[0].size),
        20,
    )(place, *[array for array, _, _ in terms], *states)
    return out[:4], out[4:]


def bits(count):
    step = 1
    while step < count:
        yield step
        step *= 2


class Grid:
    def __init__(self):
        self.fsdp = lax.axis_size("fsdp")
        self.outer = self.fsdp // CORES
        self.ctx = lax.axis_size("ctx")
        self.tensor = lax.axis_size("tensor")
        here = lax.axis_index(AXES)
        self.place = lax.rem(
            here // jnp.array([CORES * self.ctx * self.tensor, self.ctx * self.tensor, self.tensor, 1]),
            jnp.array([self.outer, CORES, self.ctx, self.tensor]),
        ).astype(jnp.int32)
        self.z = lax.axis_index("tensor")

    def index(self, fo, core, y, z):
        return ((fo * CORES + core) * self.ctx + y) * self.tensor + z

    def move(self, data, target):
        pairs = []
        for fo in range(self.outer):
            for core in range(CORES):
                for y in range(self.ctx):
                    for z in range(self.tensor):
                        pairs.append((self.index(fo, core, y, z), self.index(*target(fo, core, y, z))))
        return lax.ppermute(data, AXES, pairs)

    def swap(self, data, axis, bit=1):
        dim = ("x", "core", "y", "z").index(axis)
        return self.move(data, lambda *at: tuple(v ^ bit if i == dim else v for i, v in enumerate(at)))


def over_tensor(grid, shard):
    data = shard[None]
    for bit in reversed(list(bits(grid.tensor))):
        data = jnp.concatenate([data, grid.swap(data, "z", bit)], 0)
    return data


def axis_bits(grid, ctx_first):
    outer = [("x", bit) for bit in bits(grid.outer)]
    inner = [("y", bit) for bit in bits(grid.ctx)]
    return inner + outer if ctx_first else outer + inner


def spread(grid, planes, ctx_first):
    data, high = None, planes[None]
    for axis, bit in axis_bits(grid, ctx_first):
        data = high if data is None else jnp.concatenate([data, high], 0)
        high = grid.swap(data, axis, bit)
    far_low = grid.swap(data, "core")
    far_high = grid.swap(high, "core")
    return data, high, far_low, far_high


def collect(grid, parts, ctx_first):
    low, high, give_low, give_high = parts
    high_terms = [high, grid.swap(give_high, "core")]
    terms = [low, grid.swap(give_low, "core")]
    for step, (axis, bit) in enumerate(reversed(axis_bits(grid, ctx_first))):
        if step > 0:
            half = len_of(terms) // 2
            high_terms = [term[half : 2 * half] for term in terms]
        out = total_of(high_terms).astype(bf16)
        if step > 0:
            terms = list(terms)
        terms = terms + [grid.swap(out, axis, bit)]
    return [(term, (0,)) for term in terms]


def len_of(terms):
    return min(term.shape[0] for term in terms)


def total_of(terms):
    return sum(term.astype(f32) for term in terms)


def sum_everywhere(grid, rows):
    rows = rows + grid.swap(rows, "core")
    for axis, count in (("x", grid.outer), ("y", grid.ctx), ("z", grid.tensor)):
        for bit in bits(count):
            rows = rows + grid.swap(rows, axis, bit)
    return rows


def cross(grid, data):
    return grid.move(data, lambda f, c, y, z: (f, y, c, z))


def clips_in(grid, frames):
    frames = cross(grid, frames)

    def clip(j):
        return lax.dynamic_index_in_dim(frames, grid.z ^ j, 0, True)

    two = grid.swap(jnp.concatenate([clip(2), clip(3)], 0), "z", 2)
    one = grid.swap(jnp.concatenate([clip(1), two[1:]], 0), "z", 1)
    data = jnp.concatenate([clip(0), two[:1], one], 0)
    return data.reshape(-1, data.shape[-1])


def clips_out(grid, rows, kind, name, early):
    data = rows.reshape(grid.tensor, -1, rows.shape[-1])
    if early:
        data = cross(grid, data)
    one = grid.swap(data[2:], "z", 1)
    two = grid.swap(jnp.concatenate([data[1:2], one[1:]], 0), "z", 2)
    parts = [data[:1], one[:1], two]
    if not early:
        parts = [cross(grid, jnp.concatenate(parts, 0))]

    def body(place, *refs):
        j = 0
        for ref in refs[:-1]:
            for row in range(ref.shape[0]):
                refs[-1][pl.ds(place[3] ^ j, 1)] = ref[row : row + 1].astype(kind)
                j += 1

    first = [each.shape if len(parts) == 1 else (min(each.shape[0], 2),) + each.shape[1:] for each in parts]
    return call(
        body,
        name,
        (1,),
        [whole(*shape) for shape in first],
        whole(*data.shape),
        jax.ShapeDtypeStruct(data.shape, kind),
        [],
        0,
        0,
        8 * data.size,
        10,
    )(grid.place, *parts)


def step_of(
    frames_in,
    out_cotangent,
    attend_weight,
    output_weight,
    up_weight,
    down_weight,
    vectors,
    attend_mean,
    attend_square,
    output_mean,
    output_square,
    up_mean,
    up_square,
    down_mean,
    down_square,
    vector_mean,
    vector_square,
):
    grid = Grid()
    place = grid.place
    part = attend_weight.shape[2]
    layout = Layout(grid.outer, grid.ctx, up_weight.shape[0])

    shard = jnp.concatenate([attend_weight.astype(bf16), output_weight.astype(bf16).T[None]], 0)
    proj = over_tensor(grid, shard)
    proj = jnp.concatenate([proj[j] for j in range(grid.tensor)], 2)
    x_low = clips_in(grid, frames_in)
    proj_pieces = spread(grid, proj[:2], True) + spread(grid, proj[2:], False)
    shard = jnp.stack([up_weight.astype(bf16), down_weight.astype(bf16).T])
    ff = over_tensor(grid, shard)
    ff_pieces = spread(grid, ff[:, 0], True) + spread(grid, ff[:, 1], False)
    cot_low = clips_in(grid, out_cotangent)

    in_norm1, queries, own, weights = project(
        layout, grid.tensor, place, x_low, proj_pieces, vectors
    )
    far = grid.swap(own, "core")
    context, log_total = attend_forward(place, queries, own, far)
    residual, in_norm2 = mix(place, x_low, context, weights, vectors)
    result, dnorm2, *grads, grad_c1 = hidden_both(
        layout, place, in_norm2, cot_low, residual, ff_pieces, vectors[8:12], vectors[7]
    )
    ff_a = collect(grid, grads[:4], True)
    ff_b = collect(grid, grads[4:], False)
    frames_out = clips_out(grid, result, bf16, "y_out", False)

    dresidual, dres_low, dcontext, mid_sums = unmix(
        place, dnorm2, residual, cot_low, weights, vectors
    )
    dquery, dkeep, dgive, sums = attend_backward(
        place, queries, own, far, context, dcontext, log_total
    )
    din = grid.swap(dgive, "core")
    dproj, *grads = weigh(layout, place, in_norm1, dquery, dkeep, din, dres_low, context)
    proj_a = collect(grid, grads[:4], True)
    proj_b = collect(grid, grads[4:], False)
    dinputs, vector_part = finish(
        place, dproj, weights, x_low, dresidual, vectors, [mid_sums, sums, grad_c1], grid.tensor
    )
    frames_grad = clips_out(grid, dinputs, f32, "dx_out", True)
    vector_grad = sum_everywhere(grid, vector_part)

    groups = [ff_a, ff_b]
    arrived = []
    count = grid.tensor
    for bit in bits(grid.tensor):
        count //= 2
        name = f"gff_z{bit}"
        send = [[(a, at, (1, count)) for a, at in group] for group in groups]
        for a, _ in arrived:
            for g, group in enumerate(send):
                group.append((a, (g,), (1, count)))
        data = merge(place, name, send)
        arrived.append((grid.swap(data, "z", bit), None))
    terms = [[(a, at, (0, 1)) for a, at in group] for group in groups]
    for g, group in enumerate(terms):
        group += [(a, (g,), (0, 1)) for a, _ in arrived]
    ups, downs = update_both(
        place,
        "update_ff",
        terms,
        None,
        lambda up, down: (up[0], down[0]),
        (up_weight, up_mean, up_square),
        (down_weight.T, down_mean.T, down_square.T),
    )
    up_grad, up_new, up_mean_new, up_square_new = ups
    down_grad, down_new, down_mean_new, down_square_new = [each.T for each in downs]

    groups = [proj_a, proj_b]
    arrived = []
    count = grid.tensor
    for bit in bits(grid.tensor):
        count //= 2
        name = f"gproj_z{bit}"
        send = [[(a, at, None) for a, at in group] for group in groups]
        for a in arrived:
            for g, group in enumerate(send):
                group.append((a, (), (g, 2)))
        data = merge(place, name, send, slice(count * part, 2 * count * part))
        arrived.append(grid.swap(data, "z", bit))
    terms = [[(a, at, None) for a, at in group] for group in groups]
    for g, group in enumerate(terms):
        group += [(a, (), (g, 2)) for a in arrived]
    attends, outputs = update_both(
        place,
        "update_proj",
        terms,
        part,
        lambda one, two: (jnp.concatenate([one, two[:1]], 0), two[1].T),
        (attend_weight, attend_mean, attend_square),
        (output_weight, output_mean, output_square),
    )
    attend_grad, attend_new, attend_mean_new, attend_square_new = attends
    output_grad, output_new, output_mean_new, output_square_new = outputs
    vector_new, vector_mean_new, vector_square_new = adamw(
        vectors, vector_grad, vector_mean, vector_square, 0.0
    )
    return (
        frames_out,
        frames_grad,
        attend_grad,
        output_grad,
        up_grad,
        down_grad,
        vector_grad,
        attend_new,
        output_new,
        up_new,
        down_new,
        vector_new,
        attend_mean_new,
        attend_square_new,
        output_mean_new,
        output_square_new,
        up_mean_new,
        up_square_new,
        down_mean_new,
        down_square_new,
        vector_mean_new,
        vector_square_new,
    )


def solution(mesh):
    frames = P("fsdp", ("ctx", "tensor"), None)
    attend = P(None, ("fsdp", "ctx"), "tensor")
    tall = P("tensor", ("fsdp", "ctx"))
    flat = P(("fsdp", "ctx"), "tensor")
    weights = (attend, tall, flat, tall)
    return jax.shard_map(
        step_of,
        mesh=mesh,
        in_specs=(frames, frames)
        + weights
        + (P(), attend, attend, tall, tall, flat, flat, tall, tall, P(), P()),
        out_specs=(frames, frames)
        + weights
        + (P(),)
        + weights
        + (P(), attend, attend, tall, tall, flat, flat, tall, tall, P(), P()),
        check_vma=False,
    )
```
